32 devices in a mesh: ctx: 2 (over x), hs: 16 (over z, y, core).
Axes of the slice: x: 2, y: 2, z: 4, core: 2. Of those that a mesh axis runs over, the one named last changes fastest.
Arguments:
- key_rows: bfloat16 [16, 1024, 512], P('hs', 'ctx'), may hold values from -6 to 6
- value_rows: bfloat16 [16, 1024, 512], P('hs', 'ctx'), may hold values from -6 to 6
- query_rows: bfloat16 [16, 1024, 512], P('hs', 'ctx'), may hold values from -6 to 6
- step_rates: float32 [16, 1024], P('hs', 'ctx'), may hold values from 0.0003 to 0.003
- fast_gate: bfloat16 [16, 512, 512], P('hs', 'ctx'), may hold values from -0.25 to 0.25
- fast_up: bfloat16 [16, 512, 512], P('hs', 'ctx'), may hold values from -0.25 to 0.25
- fast_down: bfloat16 [16, 512, 512], P('hs', 'ctx'), may hold values from -0.25 to 0.25
- out_gain: float32 [2048], replicated, may hold values from 0.1 to 1.9
- gate_input: bfloat16 [1024, 4, 2048], P(('ctx', 'hs')), may hold values from -6 to 6
- out_weight: bfloat16 [2048, 1024], P('hs'), may hold values from -0.125 to 0.125
Outputs:
- layer_out: bfloat16 [1024, 4, 1024], P(('ctx', 'hs'))
The draws below stay inside these ranges and needn't reach their ends.
All inputs are finite; a program needn't handle non-finite values.
Results may differ from the reference program's by a relative error of at most 0.01.
Values may be sent and summed in bfloat16 or wider, within the bound.
A program may use at most 64 MiB of HBM per device.

```python
import math
import jax
import jax.numpy as jnp
from jax import lax

D = 2048
HEADS = 4
DH = 512
FH = 512
DOUT = 1024
GROUP = 1024
SEQS = 4
PAIRS = 16


def level_of(own_key, shape, shards, low, largest):
    gain, own = 1.0, jax.random.fold_in(own_key, 6)
    for position, blocks in shards:
        draws = jnp.exp(jax.random.uniform(jax.random.fold_in(own, position), (blocks,), jnp.float32, low / len(shards), largest / len(shards)))
        gain = gain * jnp.repeat(draws, shape[position] // blocks).reshape([-1 if axis == position else 1 for axis in range(len(shape))])
    return gain


def centred(key, extent, scale, limit, pieces=(), dtype=jnp.bfloat16):
    drawn = jax.random.normal(key, extent, jnp.float32) * scale
    if len(pieces) > 0:
        drawn = level_of(key, extent, pieces, -0.22, 0.18) * drawn
    return jnp.clip(drawn, min=-limit, max=limit).astype(dtype)


def setup_inputs(seed: int = 0) -> dict:
    arg_keys = jax.random.split(jax.random.key(seed), 11)
    key_rows = centred(arg_keys[0], (PAIRS, GROUP, DH), 1.0, 6.0, ((0, 16), (1, 2)))
    value_rows = centred(arg_keys[1], (PAIRS, GROUP, DH), 1.0, 6.0, ((0, 16), (1, 2)))
    query_rows = centred(arg_keys[2], (PAIRS, GROUP, DH), 1.0, 6.0, ((0, 16), (1, 2)))
    step_rates = jnp.clip(jnp.exp(math.log(0.003) - 2.3025851 * jax.random.uniform(arg_keys[3], (PAIRS, GROUP), jnp.float32) ** level_of(arg_keys[3], (PAIRS, GROUP), ((0, 16), (1, 2)), -0.2, 0.2)), 0.0003, 0.003)
    fast_gate = centred(arg_keys[4], (PAIRS, FH, DH), DH ** -0.5, 0.25, ((0, 16), (1, 2)))
    fast_up = centred(arg_keys[5], (PAIRS, FH, DH), DH ** -0.5, 0.25, ((0, 16), (1, 2)))
    fast_down = centred(arg_keys[6], (PAIRS, DH, FH), FH ** -0.5, 0.25, ((0, 16), (1, 2)))
    out_gain = jnp.clip(1.0 + 0.18 * jax.random.normal(arg_keys[7], (D,), jnp.float32), 0.1, 1.9)
    gate_input = centred(arg_keys[8], (GROUP, SEQS, D), 1.0, 6.0, ((0, 32),))
    out_weight = centred(arg_keys[9], (D, DOUT), D ** -0.5, 0.125, ((0, 16),))
    return dict(key_rows=key_rows, value_rows=value_rows, query_rows=query_rows, step_rates=step_rates, fast_gate=fast_gate, fast_up=fast_up, fast_down=fast_down, out_gain=out_gain, gate_input=gate_input, out_weight=out_weight)


epsilon = 1e-06

def rescale_rows(weight, update):
    base = weight.astype(jnp.float32)
    moved = base + update
    factor = jnp.sqrt(lax.optimization_barrier(jnp.mean(base * base, -1, keepdims=True)) + epsilon) / jnp.sqrt(lax.optimization_barrier(jnp.mean(moved * moved, -1, keepdims=True)) + epsilon)
    return (moved * factor).astype(jnp.bfloat16)

def inner_rows(left, right):
    return lax.dot_general(left, right, (((0,), (0,)), ((), ())), preferred_element_type=jnp.float32)

def one_pair(packed):
    key_row, value_row, query_row, rate_row, gate_fast, up_fast, down_fast = packed
    pre_gate = jnp.dot(key_row, gate_fast.T, preferred_element_type=jnp.float32)
    pre_up = jnp.dot(key_row, up_fast.T, preferred_element_type=jnp.float32)
    sig_gate = jax.nn.sigmoid(pre_gate)
    act_gate = pre_gate * sig_gate
    hidden = (act_gate * pre_up).astype(jnp.bfloat16)
    scaled = (rate_row[:, None] * value_row.astype(jnp.float32)).astype(jnp.bfloat16)
    grad_down = inner_rows(scaled, hidden)
    back_hidden = jnp.dot(scaled, down_fast, preferred_element_type=jnp.float32)
    back_gate = (back_hidden * pre_up * sig_gate * (1.0 + pre_gate * (1.0 - sig_gate))).astype(jnp.bfloat16)
    back_up = (back_hidden * act_gate).astype(jnp.bfloat16)
    grad_gate = inner_rows(back_gate, key_row)
    grad_up = inner_rows(back_up, key_row)
    new_gate = rescale_rows(gate_fast, grad_gate)
    new_up = rescale_rows(up_fast, grad_up)
    new_down = rescale_rows(down_fast, grad_down)
    query_gate = jnp.dot(query_row, new_gate.T, preferred_element_type=jnp.float32)
    query_up = jnp.dot(query_row, new_up.T, preferred_element_type=jnp.float32)
    query_hidden = (jax.nn.silu(query_gate) * query_up).astype(jnp.bfloat16)
    return jnp.dot(query_hidden, new_down.T, preferred_element_type=jnp.float32).astype(jnp.bfloat16)

def reference(key_rows, value_rows, query_rows, step_rates, fast_gate, fast_up, fast_down, out_gain, gate_input, out_weight):
    head_out = lax.map(one_pair, (key_rows, value_rows, query_rows, step_rates, fast_gate, fast_up, fast_down))
    mixed = head_out.reshape(SEQS, HEADS, GROUP, DH).transpose(2, 0, 1, 3).astype(jnp.float32)
    square = lax.optimization_barrier(jnp.mean(mixed * mixed, -1, keepdims=True))
    scaled_heads = mixed * lax.rsqrt(square + epsilon) * out_gain.reshape(HEADS, DH)
    normed = (scaled_heads.reshape(GROUP, SEQS, D) * jax.nn.silu(gate_input.astype(jnp.float32))).astype(jnp.bfloat16)
    result = jnp.dot(normed.reshape(GROUP * SEQS, D), out_weight, preferred_element_type=jnp.float32)
    return result.astype(jnp.bfloat16).reshape(GROUP, SEQS, DOUT)
```

```python
import functools

import jax
import jax.numpy as jnp
from jax import lax
from jax.experimental import pallas as pl
from jax.experimental.pallas import tpu as pltpu
from jax.sharding import PartitionSpec as P

epsilon = 1e-06


def rescale_rows(weight, update):
    base = weight.astype(jnp.float32)
    moved = base + update
    factor = jnp.sqrt(jnp.mean(base * base, -1, keepdims=True) + epsilon) / jnp.sqrt(
        jnp.mean(moved * moved, -1, keepdims=True) + epsilon
    )
    return (moved * factor).astype(jnp.bfloat16)


def inner_rows(left, right):
    return lax.dot_general(
        left, right, (((0,), (0,)), ((), ())), preferred_element_type=jnp.float32
    )


def body(
    key_rows,
    value_rows,
    query_rows,
    step_rates,
    fast_gate,
    fast_up,
    fast_down,
    out_gain,
    gate_input,
    out_weight,
):
    key_row = key_rows[0]
    value_row = value_rows[0]
    query_row = query_rows[0]
    rate_row = step_rates[0]
    whole_gate, whole_up, whole_down = (
        lax.all_gather(fast_gate, "ctx", axis=1, tiled=True),
        lax.all_gather(fast_up, "ctx", axis=1, tiled=True),
        lax.all_gather(fast_down, "ctx", axis=1, tiled=True),
    )
    gate_fast = whole_gate[0]
    up_fast = whole_up[0]
    down_fast = whole_down[0]
    pre_gate = jnp.dot(key_row, gate_fast.T, preferred_element_type=jnp.float32)
    pre_up = jnp.dot(key_row, up_fast.T, preferred_element_type=jnp.float32)
    sig_gate = jax.nn.sigmoid(pre_gate)
    act_gate = pre_gate * sig_gate
    hidden = (act_gate * pre_up).astype(jnp.bfloat16)
    scaled = (rate_row[:, None] * value_row.astype(jnp.float32)).astype(jnp.bfloat16)
    grad_down = inner_rows(scaled, hidden)
    back_hidden = jnp.dot(scaled, down_fast, preferred_element_type=jnp.float32)
    back_gate = (back_hidden * pre_up * sig_gate * (1.0 + pre_gate * (1.0 - sig_gate))).astype(
        jnp.bfloat16
    )
    back_up = (back_hidden * act_gate).astype(jnp.bfloat16)
    grad_gate = inner_rows(back_gate, key_row)
    grad_up = inner_rows(back_up, key_row)
    grad_gate, grad_up, grad_down = (
        lax.psum_scatter(grad_gate, "ctx", scatter_dimension=0, tiled=True),
        lax.psum_scatter(grad_up, "ctx", scatter_dimension=0, tiled=True),
        lax.psum_scatter(grad_down, "ctx", scatter_dimension=0, tiled=True),
    )
    part_gate = rescale_rows(fast_gate[0], grad_gate)
    part_up = rescale_rows(fast_up[0], grad_up)
    part_down = rescale_rows(fast_down[0], grad_down)
    new_gate, new_up, new_down = (
        lax.all_gather(part_gate, "ctx", axis=0, tiled=True),
        lax.all_gather(part_up, "ctx", axis=0, tiled=True),
        lax.all_gather(part_down, "ctx", axis=0, tiled=True),
    )
    query_gate = jnp.dot(query_row, new_gate.T, preferred_element_type=jnp.float32)
    query_up = jnp.dot(query_row, new_up.T, preferred_element_type=jnp.float32)
    query_hidden = (jax.nn.silu(query_gate) * query_up).astype(jnp.bfloat16)
    head_out = jnp.dot(query_hidden, new_down.T, preferred_element_type=jnp.float32).astype(
        jnp.bfloat16
    )
    width_hs = lax.axis_size("hs")
    head_size = head_out.shape[1]
    token_count = head_out.shape[0] // width_hs
    blocks = head_out.reshape(width_hs, token_count, head_size)
    moved = lax.all_to_all(blocks, "hs", split_axis=0, concat_axis=2, tiled=True)
    seq_count = gate_input.shape[1]
    model_width = gate_input.shape[2]
    head_count = model_width // head_size
    mixed = moved.reshape(token_count, seq_count, head_count, head_size).astype(jnp.float32)
    square = jnp.mean(mixed * mixed, -1, keepdims=True)
    scaled_heads = mixed * lax.rsqrt(square + epsilon) * out_gain.reshape(head_count, head_size)
    normed = (
        scaled_heads.reshape(token_count, seq_count, model_width)
        * jax.nn.silu(gate_input.astype(jnp.float32))
    ).astype(jnp.bfloat16)
    flat_rows = normed.reshape(token_count * seq_count, model_width)
    out_cols = out_weight.shape[1]
    full_weight = lax.all_gather(out_weight, "hs", axis=0, tiled=True)
    result = jnp.dot(flat_rows, full_weight, preferred_element_type=jnp.float32)
    return result.astype(jnp.bfloat16).reshape(token_count, seq_count, out_cols)


MESH = pl.DeviceIdType.MESH


def inner_cols(left, right):
    return lax.dot_general(
        left, right, (((1,), (1,)), ((), ())), preferred_element_type=jnp.float32
    )


def layer_kernel(
    layers,
    pieces,
    gate_hbm,
    up_hbm,
    down_hbm,
    key_hbm,
    scaled_hbm,
    query_hbm,
    side_hbm,
    weight_hbm,
    gain_ref,
    out_ref,
    fast,
    fresh,
    keys,
    scaled,
    queries,
    side,
    full,
    grads,
    heads,
    mixed,
    normed,
    local_sem,
    ctx_send,
    ctx_recv,
    full_send,
    full_recv,
    head_send,
    head_recv,
):
    ctx = lax.axis_index("ctx")
    me = lax.axis_index("hs")
    other = 1 - ctx
    count = 4 * layers
    depth, inner = me // 4, me % 4
    row, core = inner // 2, inner % 2
    row_peer = depth * 4 + (1 - row) * 2 + core
    core_peer = depth * 4 + row * 2 + (1 - core)

    def remote(source, target, send, recv, device):
        return pltpu.make_async_remote_copy(
            src_ref=source,
            dst_ref=target,
            send_sem=send,
            recv_sem=recv,
            device_id=device,
            device_id_type=MESH,
        )

    part = gate_hbm.shape[1]
    tokens = key_hbm.shape[1]
    piece = tokens // pieces
    shard = weight_hbm.shape[0]

    def rows(start, size):
        return pl.ds(pl.multiple_of(start, size), size)

    weights = (gate_hbm, up_hbm, down_hbm)
    local = []
    for i, source in enumerate(weights):
        local.append(
            pltpu.make_async_copy(source.at[0], fast.at[i, rows(ctx * part, part)], local_sem.at[i])
        )
    local.append(
        pltpu.make_async_copy(key_hbm.at[0], keys.at[rows(ctx * tokens, tokens)], local_sem.at[3])
    )
    local.append(
        pltpu.make_async_copy(scaled_hbm, scaled.at[rows(ctx * tokens, tokens)], local_sem.at[4])
    )
    local.append(pltpu.make_async_copy(weight_hbm, full.at[rows(me * shard, shard)], local_sem.at[5]))
    local.append(pltpu.make_async_copy(query_hbm.at[0], queries, local_sem.at[6]))
    local.append(pltpu.make_async_copy(side_hbm, side, local_sem.at[7]))
    for copy in local:
        copy.start()

    barrier = pltpu.get_barrier_semaphore()
    pl.semaphore_signal(barrier, inc=1, device_id={"ctx": other}, device_id_type=MESH)
    for step in range(1, count):
        pl.semaphore_signal(
            barrier, inc=1, device_id={"hs": (me + step) % count}, device_id_type=MESH
        )
    pl.semaphore_wait(barrier, count)

    swaps = []
    for i, source in enumerate(weights):
        swaps.append((source.at[0], lambda who, i=i: fast.at[i, rows(who * part, part)]))
    for j in range(pieces):
        for source, target in ((key_hbm.at[0], keys), (scaled_hbm, scaled)):
            swaps.append(
                (
                    source.at[pl.ds(j * piece, piece)],
                    lambda who, target=target, j=j: target.at[
                        rows(who * tokens + j * piece, piece)
                    ],
                )
            )
    outgoing = [
        remote(source, target(ctx), ctx_send.at[i], ctx_recv.at[i], {"ctx": other})
        for i, (source, target) in enumerate(swaps)
    ]
    incoming = [
        remote(source, target(other), ctx_send.at[i], ctx_recv.at[i], {"ctx": other})
        for i, (source, target) in enumerate(swaps)
    ]
    for copy in outgoing:
        copy.start()

    sent = []

    def forward(source, index, device):
        slot = full_send.at[len(sent)]
        copy = remote(
            source, full.at[rows(index * shard, shard)], slot, full_recv.at[index], {"hs": device}
        )
        copy.start()
        sent.append(copy)

    def arrived(index):
        block = full.at[rows(index * shard, shard)]
        remote(block, block, full_send.at[0], full_recv.at[index], {"hs": core_peer}).wait_recv()
        return block

    for step in range(1, layers):
        forward(weight_hbm, me, ((depth + step) % layers) * 4 + inner)
    forward(weight_hbm, me, row_peer)
    forward(weight_hbm, me, core_peer)

    def learn(start, first):
        key_part = keys[rows(start, piece), :]
        scaled_part = scaled[rows(start, piece), :]
        pre_gate = inner_cols(key_part, fast[0])
        pre_up = inner_cols(key_part, fast[1])
        sig_gate = jax.nn.sigmoid(pre_gate)
        act_gate = pre_gate * sig_gate
        hidden = (act_gate * pre_up).astype(jnp.bfloat16)
        back_hidden = jnp.dot(scaled_part, fast[2], preferred_element_type=jnp.float32)
        back_gate = (
            back_hidden * pre_up * sig_gate * (1.0 + pre_gate * (1.0 - sig_gate))
        ).astype(jnp.bfloat16)
        back_up = (back_hidden * act_gate).astype(jnp.bfloat16)
        terms = (
            inner_rows(back_gate, key_part),
            inner_rows(back_up, key_part),
            inner_rows(scaled_part, hidden),
        )
        for i, term in enumerate(terms):
            grads[i] = term if first else grads[i] + term

    for copy in local[:5]:
        copy.wait()
    for copy in incoming[:3]:
        copy.wait_recv()
    for j in range(pieces):
        learn(ctx * tokens + j * piece, j == 0)

    for step in range(1, layers):
        index = ((depth + layers - step) % layers) * 4 + inner
        block = arrived(index)
        forward(block, index, row_peer)
        forward(block, index, core_peer)

    for j in range(pieces):
        if j == pieces - 1:
            for step in range(layers):
                index = ((depth + layers - step) % layers) * 4 + (1 - row) * 2 + core
                forward(arrived(index), index, core_peer)
        incoming[3 + 2 * j].wait_recv()
        incoming[4 + 2 * j].wait_recv()
        learn(other * tokens + j * piece, False)

    for i in range(3):
        fresh[i] = rescale_rows(fast[i], grads[i])

    local[6].wait()
    block_rows = tokens // count
    step_rows = 4 * block_rows
    copies = []
    for step in range(1, layers + 1):
        target = (depth + step) % layers
        query_part = queries[rows(target * step_rows, step_rows), :]
        query_gate = inner_cols(query_part, fresh[0])
        query_up = inner_cols(query_part, fresh[1])
        query_hidden = (query_gate * jax.nn.sigmoid(query_gate) * query_up).astype(jnp.bfloat16)
        head_part = inner_cols(query_hidden, fresh[2]).astype(jnp.bfloat16)
        heads[rows(target * step_rows, step_rows), :] = head_part
        for i in range(4):
            device = target * 4 + (inner + i) % 4
            source = heads.at[rows(device * block_rows, block_rows)]
            if step == layers and i == 0:
                mixed[me] = source[...]
            else:
                slot = len(copies)
                copy = remote(
                    source, mixed.at[me], head_send.at[slot], head_recv.at[me], {"hs": device}
                )
                copy.start()
                copies.append(copy)

    for copy in (local[5], local[7]):
        copy.wait()
    for step in range(layers):
        for other_row in range(2):
            arrived(((depth + step) % layers) * 4 + ((row + other_row) % 2) * 2 + (1 - core))
    for copy in outgoing + sent:
        copy.wait_send()
    for step in range(1, count):
        index = (me + step) % count
        remote(
            heads.at[pl.ds(0, block_rows)],
            mixed.at[index],
            head_send.at[0],
            head_recv.at[index],
            {"hs": core_peer},
        ).wait_recv()
    for copy in copies:
        copy.wait_send()

    size = mixed.shape[2]
    head_count = side.shape[2] // size
    for seq in range(side.shape[0]):
        for head in range(head_count):
            columns = slice(head * size, (head + 1) * size)
            value = mixed[seq * head_count + head].astype(jnp.float32)
            square = jnp.mean(value * value, -1, keepdims=True)
            value = value * lax.rsqrt(square + epsilon) * gain_ref[:, columns]
            gate = side[seq, :, columns].astype(jnp.float32)
            normed[seq * block_rows : (seq + 1) * block_rows, columns] = (
                value * (gate * jax.nn.sigmoid(gate))
            ).astype(jnp.bfloat16)
    result = jnp.dot(normed[...], full[...], preferred_element_type=jnp.float32)
    for seq in range(side.shape[0]):
        out_ref[seq] = result[seq * block_rows : (seq + 1) * block_rows].astype(jnp.bfloat16)


def swapped_body(
    key_rows,
    value_rows,
    query_rows,
    step_rates,
    fast_gate,
    fast_up,
    fast_down,
    out_gain,
    gate_input,
    out_weight,
):
    layers = lax.axis_size("hs") // 4
    count = 4 * layers
    pieces = 2
    tokens, size = key_rows.shape[1:]
    hidden_size = 2 * fast_gate.shape[1]
    block_rows, seq_count, width = gate_input.shape
    columns = out_weight.shape[1]
    scaled = (step_rates[0][:, None] * value_rows[0].astype(jnp.float32)).astype(jnp.bfloat16)
    side = gate_input.transpose(1, 0, 2)
    anywhere = pl.BlockSpec(memory_space=pl.ANY)
    inside = pl.BlockSpec(memory_space=pltpu.VMEM)
    half = jnp.bfloat16
    result = pl.pallas_call(
        functools.partial(layer_kernel, layers, pieces),
        out_shape=jax.ShapeDtypeStruct((seq_count, block_rows, columns), half),
        in_specs=[anywhere] * 8 + [inside],
        out_specs=inside,
        scratch_shapes=[
            pltpu.VMEM((3, hidden_size, size), half),
            pltpu.VMEM((3, hidden_size, size), half),
            pltpu.VMEM((2 * tokens, size), half),
            pltpu.VMEM((2 * tokens, size), half),
            pltpu.VMEM((tokens, size), half),
            pltpu.VMEM((seq_count, block_rows, width), half),
            pltpu.VMEM((width, columns), half),
            pltpu.VMEM((3, hidden_size, size), jnp.float32),
            pltpu.VMEM((tokens, size), half),
            pltpu.VMEM((count, block_rows, size), half),
            pltpu.VMEM((seq_count * block_rows, width), half),
            pltpu.SemaphoreType.DMA((8,)),
            pltpu.SemaphoreType.DMA((3 + 2 * pieces,)),
            pltpu.SemaphoreType.DMA((3 + 2 * pieces,)),
            pltpu.SemaphoreType.DMA((4 * layers,)),
            pltpu.SemaphoreType.DMA((count,)),
            pltpu.SemaphoreType.DMA((count,)),
            pltpu.SemaphoreType.DMA((count,)),
        ],
        compiler_params=pltpu.CompilerParams(
            collective_id=0, has_side_effects=True, vmem_limit_bytes=60 * 1024 * 1024
        ),
    )(
        fast_gate,
        fast_up,
        fast_down,
        key_rows,
        scaled,
        query_rows,
        side,
        out_weight,
        out_gain[None],
    )
    return result.transpose(1, 0, 2)


def solution(mesh):
    def step(*arrays):
        paired = mesh.shape["ctx"] == 2 and mesh.shape["hs"] % 4 == 0
        paired = paired and arrays[0].shape[0] == 1
        return (swapped_body if paired else body)(*arrays)

    return jax.shard_map(
        step,
        mesh=mesh,
        in_specs=(
            P("hs", "ctx", None),
            P("hs", "ctx", None),
            P("hs", "ctx", None),
            P("hs", "ctx"),
            P("hs", "ctx", None),
            P("hs", "ctx", None),
            P("hs", "ctx", None),
            P(),
            P(("ctx", "hs"), None, None),
            P("hs", None),
        ),
        out_specs=P(("ctx", "hs"), None, None),
        check_vma=False,
    )
```

```python
import functools

import jax
import jax.numpy as jnp
from jax import lax
from jax.experimental import pallas as pl
from jax.experimental.pallas import tpu as pltpu
from jax.sharding import PartitionSpec as P

epsilon = 1e-06


def rescale_rows(weight, update):
    base = weight.astype(jnp.float32)
    moved = base + update
    factor = jnp.sqrt(jnp.mean(base * base, -1, keepdims=True) + epsilon) / jnp.sqrt(
        jnp.mean(moved * moved, -1, keepdims=True) + epsilon
    )
    return (moved * factor).astype(jnp.bfloat16)


def inner_rows(left, right):
    return lax.dot_general(
        left, right, (((0,), (0,)), ((), ())), preferred_element_type=jnp.float32
    )


def body(
    key_rows,
    value_rows,
    query_rows,
    step_rates,
    fast_gate,
    fast_up,
    fast_down,
    out_gain,
    gate_input,
    out_weight,
):
    key_row = key_rows[0]
    value_row = value_rows[0]
    query_row = query_rows[0]
    rate_row = step_rates[0]
    whole_gate, whole_up, whole_down = (
        lax.all_gather(fast_gate, "ctx", axis=1, tiled=True),
        lax.all_gather(fast_up, "ctx", axis=1, tiled=True),
        lax.all_gather(fast_down, "ctx", axis=1, tiled=True),
    )
    gate_fast = whole_gate[0]
    up_fast = whole_up[0]
    down_fast = whole_down[0]
    pre_gate = jnp.dot(key_row, gate_fast.T, preferred_element_type=jnp.float32)
    pre_up = jnp.dot(key_row, up_fast.T, preferred_element_type=jnp.float32)
    sig_gate = jax.nn.sigmoid(pre_gate)
    act_gate = pre_gate * sig_gate
    hidden = (act_gate * pre_up).astype(jnp.bfloat16)
    scaled = (rate_row[:, None] * value_row.astype(jnp.float32)).astype(jnp.bfloat16)
    grad_down = inner_rows(scaled, hidden)
    back_hidden = jnp.dot(scaled, down_fast, preferred_element_type=jnp.float32)
    back_gate = (back_hidden * pre_up * sig_gate * (1.0 + pre_gate * (1.0 - sig_gate))).astype(
        jnp.bfloat16
    )
    back_up = (back_hidden * act_gate).astype(jnp.bfloat16)
    grad_gate = inner_rows(back_gate, key_row)
    grad_up = inner_rows(back_up, key_row)
    grad_gate, grad_up, grad_down = (
        lax.psum_scatter(grad_gate, "ctx", scatter_dimension=0, tiled=True),
        lax.psum_scatter(grad_up, "ctx", scatter_dimension=0, tiled=True),
        lax.psum_scatter(grad_down, "ctx", scatter_dimension=0, tiled=True),
    )
    part_gate = rescale_rows(fast_gate[0], grad_gate)
    part_up = rescale_rows(fast_up[0], grad_up)
    part_down = rescale_rows(fast_down[0], grad_down)
    new_gate, new_up, new_down = (
        lax.all_gather(part_gate, "ctx", axis=0, tiled=True),
        lax.all_gather(part_up, "ctx", axis=0, tiled=True),
        lax.all_gather(part_down, "ctx", axis=0, tiled=True),
    )
    query_gate = jnp.dot(query_row, new_gate.T, preferred_element_type=jnp.float32)
    query_up = jnp.dot(query_row, new_up.T, preferred_element_type=jnp.float32)
    query_hidden = (jax.nn.silu(query_gate) * query_up).astype(jnp.bfloat16)
    head_out = jnp.dot(query_hidden, new_down.T, preferred_element_type=jnp.float32).astype(
        jnp.bfloat16
    )
    width_hs = lax.axis_size("hs")
    head_size = head_out.shape[1]
    token_count = head_out.shape[0] // width_hs
    blocks = head_out.reshape(width_hs, token_count, head_size)
    moved = lax.all_to_all(blocks, "hs", split_axis=0, concat_axis=2, tiled=True)
    seq_count = gate_input.shape[1]
    model_width = gate_input.shape[2]
    head_count = model_width // head_size
    mixed = moved.reshape(token_count, seq_count, head_count, head_size).astype(jnp.float32)
    square = jnp.mean(mixed * mixed, -1, keepdims=True)
    scaled_heads = mixed * lax.rsqrt(square + epsilon) * out_gain.reshape(head_count, head_size)
    normed = (
        scaled_heads.reshape(token_count, seq_count, model_width)
        * jax.nn.silu(gate_input.astype(jnp.float32))
    ).astype(jnp.bfloat16)
    flat_rows = normed.reshape(token_count * seq_count, model_width)
    out_cols = out_weight.shape[1]
    full_weight = lax.all_gather(out_weight, "hs", axis=0, tiled=True)
    result = jnp.dot(flat_rows, full_weight, preferred_element_type=jnp.float32)
    return result.astype(jnp.bfloat16).reshape(token_count, seq_count, out_cols)


MESH = pl.DeviceIdType.MESH


def inner_cols(left, right):
    return lax.dot_general(
        left, right, (((1,), (1,)), ((), ())), preferred_element_type=jnp.float32
    )


def layer_kernel(
    layers,
    pieces,
    gate_hbm,
    up_hbm,
    down_hbm,
    key_hbm,
    scaled_hbm,
    query_hbm,
    side_hbm,
    weight_hbm,
    gain_ref,
    out_ref,
    fast,
    fresh,
    keys,
    scaled,
    queries,
    side,
    full,
    grads,
    heads,
    mixed,
    normed,
    local_sem,
    ctx_send,
    ctx_recv,
    full_send,
    full_recv,
    head_send,
    head_recv,
    fresh_send,
    fresh_recv,
):
    ctx = lax.axis_index("ctx")
    me = lax.axis_index("hs")
    other = 1 - ctx
    count = 4 * layers
    depth, inner = me // 4, me % 4
    row, core = inner // 2, inner % 2
    row_peer = depth * 4 + (1 - row) * 2 + core
    core_peer = depth * 4 + row * 2 + (1 - core)
    pair = depth * 4 + row * 2 + ctx
    owner = core == ctx
    helper = core != ctx

    def remote(source, target, send, recv, device):
        return pltpu.make_async_remote_copy(
            src_ref=source,
            dst_ref=target,
            send_sem=send,
            recv_sem=recv,
            device_id=device,
            device_id_type=MESH,
        )

    part = gate_hbm.shape[1]
    tokens = key_hbm.shape[1]
    piece = tokens // pieces
    shard = weight_hbm.shape[0]

    def rows(start, size):
        return pl.ds(pl.multiple_of(start, size), size)

    weights = (gate_hbm, up_hbm, down_hbm)
    local = []
    for i, source in enumerate(weights):
        local.append(
            pltpu.make_async_copy(source.at[0], fast.at[i, rows(ctx * part, part)], local_sem.at[i])
        )
    local.append(
        pltpu.make_async_copy(key_hbm.at[0], keys.at[rows(ctx * tokens, tokens)], local_sem.at[3])
    )
    local.append(
        pltpu.make_async_copy(scaled_hbm, scaled.at[rows(ctx * tokens, tokens)], local_sem.at[4])
    )
    local.append(pltpu.make_async_copy(weight_hbm, full.at[rows(me * shard, shard)], local_sem.at[5]))
    local.append(pltpu.make_async_copy(query_hbm.at[0], queries, local_sem.at[6]))
    local.append(pltpu.make_async_copy(side_hbm, side, local_sem.at[7]))
    owned = [0, 1, 2, 3, 4, 6]
    for i in (5, 7):
        local[i].start()

    @pl.when(owner)
    def _():
        for i in owned:
            local[i].start()

    barrier = pltpu.get_barrier_semaphore()
    pl.semaphore_signal(barrier, inc=1, device_id={"ctx": other}, device_id_type=MESH)
    for step in range(1, count):
        for side_ctx in (ctx, other):
            pl.semaphore_signal(
                barrier,
                inc=1,
                device_id={"ctx": side_ctx, "hs": (me + step) % count},
                device_id_type=MESH,
            )
    pl.semaphore_wait(barrier, 2 * count - 1)

    swaps = []
    for i, source in enumerate(weights):
        swaps.append((source.at[0], lambda who, i=i: fast.at[i, rows(who * part, part)]))
    for j in range(pieces):
        for source, target in ((key_hbm.at[0], keys), (scaled_hbm, scaled)):
            swaps.append(
                (
                    source.at[pl.ds(j * piece, piece)],
                    lambda who, target=target, j=j: target.at[
                        rows(who * tokens + j * piece, piece)
                    ],
                )
            )
    outgoing = [
        remote(source, target(ctx), ctx_send.at[i], ctx_recv.at[i], {"ctx": other})
        for i, (source, target) in enumerate(swaps)
    ]
    incoming = [
        remote(source, target(other), ctx_send.at[i], ctx_recv.at[i], {"ctx": other})
        for i, (source, target) in enumerate(swaps)
    ]
    asked = remote(
        query_hbm.at[0],
        queries,
        ctx_send.at[len(swaps)],
        ctx_recv.at[len(swaps)],
        {"ctx": other, "hs": core_peer},
    )

    @pl.when(helper)
    def _():
        for copy in outgoing:
            copy.start()
        asked.start()

    def full_copy(source, index, slot, device):
        return remote(
            source,
            full.at[rows(index * shard, shard)],
            full_send.at[slot],
            full_recv.at[index],
            {"hs": device},
        )

    def arrived(index):
        block = full.at[rows(index * shard, shard)]
        remote(block, block, full_send.at[0], full_recv.at[index], {"hs": core_peer}).wait_recv()

    def held(index):
        return full.at[rows(index * shard, shard)]

    sends = [
        (depth < layers - 1, full_copy(weight_hbm, me, 0, me + 4)),
        (depth > 0, full_copy(weight_hbm, me, 1, me - 4)),
        (None, full_copy(weight_hbm, me, 2, row_peer)),
        (None, full_copy(weight_hbm, me, 3, core_peer)),
    ]

    def guarded(condition, action):
        if condition is None:
            action()
        else:
            pl.when(condition)(action)

    for condition, copy in sends:
        guarded(condition, copy.start)

    def relay(hop):
        for turn, (exists, onward) in enumerate(
            (
                (depth >= hop, depth < layers - 1),
                (depth + hop <= layers - 1, depth > 0),
            )
        ):
            index = me - 4 * hop if turn == 0 else me + 4 * hop
            slot = 4 + ((hop - 1) * 2 + turn) * 3
            next_device = me + 4 if turn == 0 else me - 4
            made = [
                (exists & onward, full_copy(held(index), index, slot, next_device)),
                (exists, full_copy(held(index), index, slot + 1, row_peer)),
                (exists, full_copy(held(index), index, slot + 2, core_peer)),
            ]
            pl.when(exists)(functools.partial(arrived, index))
            for condition, copy in made:
                guarded(condition, copy.start)
            sends.extend(made)

    crossed = []
    for step in range(layers):
        index = ((depth + step) % layers) * 4 + (1 - row) * 2 + core
        slot = 4 + 6 * (layers - 1) + step
        crossed.append((index, full_copy(held(index), index, slot, core_peer)))

    def cross():
        for index, copy in crossed:
            arrived(index)
            copy.start()

    def learn(start, first):
        key_part = keys[rows(start, piece), :]
        scaled_part = scaled[rows(start, piece), :]
        pre_gate = inner_cols(key_part, fast[0])
        pre_up = inner_cols(key_part, fast[1])
        sig_gate = jax.nn.sigmoid(pre_gate)
        act_gate = pre_gate * sig_gate
        hidden = (act_gate * pre_up).astype(jnp.bfloat16)
        back_hidden = jnp.dot(scaled_part, fast[2], preferred_element_type=jnp.float32)
        back_gate = (
            back_hidden * pre_up * sig_gate * (1.0 + pre_gate * (1.0 - sig_gate))
        ).astype(jnp.bfloat16)
        back_up = (back_hidden * act_gate).astype(jnp.bfloat16)
        terms = (
            inner_rows(back_gate, key_part),
            inner_rows(back_up, key_part),
            inner_rows(scaled_part, hidden),
        )
        for i, term in enumerate(terms):
            grads[i] = term if first else grads[i] + term

    handed = [
        remote(fresh.at[i], fresh.at[i], fresh_send.at[i], fresh_recv.at[i], {"hs": core_peer})
        for i in range(3)
    ]
    hops = list(range(1, layers))
    if hops:
        relay(hops.pop(0))

    @pl.when(owner)
    def _():
        for i in owned[:5]:
            local[i].wait()
        for copy in incoming[:3]:
            copy.wait_recv()
        for j in range(pieces):
            learn(ctx * tokens + j * piece, j == 0)

    for j in range(pieces):
        if hops:
            relay(hops.pop(0))

        @pl.when(owner)
        def _():
            incoming[3 + 2 * j].wait_recv()
            incoming[4 + 2 * j].wait_recv()
            learn(other * tokens + j * piece, False)

    for hop in hops:
        relay(hop)

    @pl.when(owner)
    def _():
        for i in range(3):
            fresh[i] = rescale_rows(fast[i], grads[i])
            handed[i].start()
        local[6].wait()

    @pl.when(helper)
    def _():
        cross()
        asked.wait_recv()
        for copy in handed:
            copy.wait_recv()

    block_rows = tokens // count
    step_rows = 4 * block_rows
    copies = []
    for step in range(1, layers + 1):
        target = (depth + step) % layers
        query_part = queries[rows(target * step_rows, step_rows), :]
        query_gate = inner_cols(query_part, fresh[0])
        query_up = inner_cols(query_part, fresh[1])
        query_hidden = (query_gate * jax.nn.sigmoid(query_gate) * query_up).astype(jnp.bfloat16)
        head_part = inner_cols(query_hidden, fresh[2]).astype(jnp.bfloat16)
        heads[rows(target * step_rows, step_rows), :] = head_part
        for i in range(4):
            device = target * 4 + (inner + i) % 4
            source = heads.at[rows(device * block_rows, block_rows)]
            slot = len(copies)
            copy = remote(
                source,
                mixed.at[pair],
                head_send.at[slot],
                head_recv.at[pair],
                {"ctx": core, "hs": device},
            )
            condition = None
            if step == layers and i == 0:
                condition = helper

                @pl.when(owner)
                def _():
                    mixed[me] = source[...]

            guarded(condition, copy.start)
            copies.append((condition, copy))

    pl.when(owner)(cross)
    for i in (5, 7):
        local[i].wait()
    for step in range(layers):
        for other_row in range(2):
            arrived(((depth + step) % layers) * 4 + ((row + other_row) % 2) * 2 + (1 - core))

    def head_arrived(index):
        remote(
            heads.at[pl.ds(0, block_rows)],
            mixed.at[index],
            head_send.at[0],
            head_recv.at[index],
            {"hs": core_peer},
        ).wait_recv()

    for step in range(1, count):
        head_arrived((me + step) % count)
    pl.when(helper)(functools.partial(head_arrived, me))

    for condition, copy in sends + copies:
        guarded(condition, copy.wait_send)
    for _, copy in crossed:
        copy.wait_send()

    @pl.when(helper)
    def _():
        for copy in outgoing:
            copy.wait_send()
        asked.wait_send()

    @pl.when(owner)
    def _():
        for copy in handed:
            copy.wait_send()

    size = mixed.shape[2]
    head_count = side.shape[2] // size
    for seq in range(side.shape[0]):
        for head in range(head_count):
            columns = slice(head * size, (head + 1) * size)
            value = mixed[seq * head_count + head].astype(jnp.float32)
            square = jnp.mean(value * value, -1, keepdims=True)
            value = value * lax.rsqrt(square + epsilon) * gain_ref[:, columns]
            gate = side[seq, :, columns].astype(jnp.float32)
            normed[seq * block_rows : (seq + 1) * block_rows, columns] = (
                value * (gate * jax.nn.sigmoid(gate))
            ).astype(jnp.bfloat16)
    result = jnp.dot(normed[...], full[...], preferred_element_type=jnp.float32)
    for seq in range(side.shape[0]):
        out_ref[seq] = result[seq * block_rows : (seq + 1) * block_rows].astype(jnp.bfloat16)


def swapped_body(
    key_rows,
    value_rows,
    query_rows,
    step_rates,
    fast_gate,
    fast_up,
    fast_down,
    out_gain,
    gate_input,
    out_weight,
):
    layers = lax.axis_size("hs") // 4
    count = 4 * layers
    pieces = 2
    tokens, size = key_rows.shape[1:]
    hidden_size = 2 * fast_gate.shape[1]
    block_rows, seq_count, width = gate_input.shape
    columns = out_weight.shape[1]
    scaled = (step_rates[0][:, None] * value_rows[0].astype(jnp.float32)).astype(jnp.bfloat16)
    side = gate_input.transpose(1, 0, 2)
    anywhere = pl.BlockSpec(memory_space=pl.ANY)
    inside = pl.BlockSpec(memory_space=pltpu.VMEM)
    half = jnp.bfloat16
    result = pl.pallas_call(
        functools.partial(layer_kernel, layers, pieces),
        out_shape=jax.ShapeDtypeStruct((seq_count, block_rows, columns), half),
        in_specs=[anywhere] * 8 + [inside],
        out_specs=inside,
        scratch_shapes=[
            pltpu.VMEM((3, hidden_size, size), half),
            pltpu.VMEM((3, hidden_size, size), half),
            pltpu.VMEM((2 * tokens, size), half),
            pltpu.VMEM((2 * tokens, size), half),
            pltpu.VMEM((tokens, size), half),
            pltpu.VMEM((seq_count, block_rows, width), half),
            pltpu.VMEM((width, columns), half),
            pltpu.VMEM((3, hidden_size, size), jnp.float32),
            pltpu.VMEM((tokens, size), half),
            pltpu.VMEM((count, block_rows, size), half),
            pltpu.VMEM((seq_count * block_rows, width), half),
            pltpu.SemaphoreType.DMA((8,)),
            pltpu.SemaphoreType.DMA((4 + 2 * pieces,)),
            pltpu.SemaphoreType.DMA((4 + 2 * pieces,)),
            pltpu.SemaphoreType.DMA((4 + 6 * (layers - 1) + layers,)),
            pltpu.SemaphoreType.DMA((count,)),
            pltpu.SemaphoreType.DMA((count,)),
            pltpu.SemaphoreType.DMA((count,)),
            pltpu.SemaphoreType.DMA((3,)),
            pltpu.SemaphoreType.DMA((3,)),
        ],
        compiler_params=pltpu.CompilerParams(
            collective_id=0, has_side_effects=True, vmem_limit_bytes=60 * 1024 * 1024
        ),
    )(
        fast_gate,
        fast_up,
        fast_down,
        key_rows,
        scaled,
        query_rows,
        side,
        out_weight,
        out_gain[None],
    )
    return result.transpose(1, 0, 2)


def solution(mesh):
    def step(*arrays):
        paired = mesh.shape["ctx"] == 2 and mesh.shape["hs"] % 4 == 0
        paired = paired and arrays[0].shape[0] == 1
        return (swapped_body if paired else body)(*arrays)

    return jax.shard_map(
        step,
        mesh=mesh,
        in_specs=(
            P("hs", "ctx", None),
            P("hs", "ctx", None),
            P("hs", "ctx", None),
            P("hs", "ctx"),
            P("hs", "ctx", None),
            P("hs", "ctx", None),
            P("hs", "ctx", None),
            P(),
            P(("ctx", "hs"), None, None),
            P("hs", None),
        ),
        out_specs=P(("ctx", "hs"), None, None),
        check_vma=False,
    )
```

```python
import functools

import jax
import jax.numpy as jnp
from jax import lax
from jax.experimental import pallas as pl
from jax.experimental.pallas import tpu as pltpu
from jax.sharding import PartitionSpec as P

epsilon = 1e-06


def rescale_rows(weight, update):
    base = weight.astype(jnp.float32)
    moved = base + update
    factor = jnp.sqrt(jnp.mean(base * base, -1, keepdims=True) + epsilon) / jnp.sqrt(
        jnp.mean(moved * moved, -1, keepdims=True) + epsilon
    )
    return (moved * factor).astype(jnp.bfloat16)


def inner_rows(left, right):
    return lax.dot_general(
        left, right, (((0,), (0,)), ((), ())), preferred_element_type=jnp.float32
    )


def body(
    key_rows,
    value_rows,
    query_rows,
    step_rates,
    fast_gate,
    fast_up,
    fast_down,
    out_gain,
    gate_input,
    out_weight,
):
    key_row = key_rows[0]
    value_row = value_rows[0]
    query_row = query_rows[0]
    rate_row = step_rates[0]
    whole_gate, whole_up, whole_down = (
        lax.all_gather(fast_gate, "ctx", axis=1, tiled=True),
        lax.all_gather(fast_up, "ctx", axis=1, tiled=True),
        lax.all_gather(fast_down, "ctx", axis=1, tiled=True),
    )
    gate_fast = whole_gate[0]
    up_fast = whole_up[0]
    down_fast = whole_down[0]
    pre_gate = jnp.dot(key_row, gate_fast.T, preferred_element_type=jnp.float32)
    pre_up = jnp.dot(key_row, up_fast.T, preferred_element_type=jnp.float32)
    sig_gate = jax.nn.sigmoid(pre_gate)
    act_gate = pre_gate * sig_gate
    hidden = (act_gate * pre_up).astype(jnp.bfloat16)
    scaled = (rate_row[:, None] * value_row.astype(jnp.float32)).astype(jnp.bfloat16)
    grad_down = inner_rows(scaled, hidden)
    back_hidden = jnp.dot(scaled, down_fast, preferred_element_type=jnp.float32)
    back_gate = (back_hidden * pre_up * sig_gate * (1.0 + pre_gate * (1.0 - sig_gate))).astype(
        jnp.bfloat16
    )
    back_up = (back_hidden * act_gate).astype(jnp.bfloat16)
    grad_gate = inner_rows(back_gate, key_row)
    grad_up = inner_rows(back_up, key_row)
    grad_gate, grad_up, grad_down = (
        lax.psum_scatter(grad_gate, "ctx", scatter_dimension=0, tiled=True),
        lax.psum_scatter(grad_up, "ctx", scatter_dimension=0, tiled=True),
        lax.psum_scatter(grad_down, "ctx", scatter_dimension=0, tiled=True),
    )
    part_gate = rescale_rows(fast_gate[0], grad_gate)
    part_up = rescale_rows(fast_up[0], grad_up)
    part_down = rescale_rows(fast_down[0], grad_down)
    new_gate, new_up, new_down = (
        lax.all_gather(part_gate, "ctx", axis=0, tiled=True),
        lax.all_gather(part_up, "ctx", axis=0, tiled=True),
        lax.all_gather(part_down, "ctx", axis=0, tiled=True),
    )
    query_gate = jnp.dot(query_row, new_gate.T, preferred_element_type=jnp.float32)
    query_up = jnp.dot(query_row, new_up.T, preferred_element_type=jnp.float32)
    query_hidden = (jax.nn.silu(query_gate) * query_up).astype(jnp.bfloat16)
    head_out = jnp.dot(query_hidden, new_down.T, preferred_element_type=jnp.float32).astype(
        jnp.bfloat16
    )
    width_hs = lax.axis_size("hs")
    head_size = head_out.shape[1]
    token_count = head_out.shape[0] // width_hs
    blocks = head_out.reshape(width_hs, token_count, head_size)
    moved = lax.all_to_all(blocks, "hs", split_axis=0, concat_axis=2, tiled=True)
    seq_count = gate_input.shape[1]
    model_width = gate_input.shape[2]
    head_count = model_width // head_size
    mixed = moved.reshape(token_count, seq_count, head_count, head_size).astype(jnp.float32)
    square = jnp.mean(mixed * mixed, -1, keepdims=True)
    scaled_heads = mixed * lax.rsqrt(square + epsilon) * out_gain.reshape(head_count, head_size)
    normed = (
        scaled_heads.reshape(token_count, seq_count, model_width)
        * jax.nn.silu(gate_input.astype(jnp.float32))
    ).astype(jnp.bfloat16)
    flat_rows = normed.reshape(token_count * seq_count, model_width)
    out_cols = out_weight.shape[1]
    full_weight = lax.all_gather(out_weight, "hs", axis=0, tiled=True)
    result = jnp.dot(flat_rows, full_weight, preferred_element_type=jnp.float32)
    return result.astype(jnp.bfloat16).reshape(token_count, seq_count, out_cols)


MESH = pl.DeviceIdType.MESH


def inner_cols(left, right):
    return lax.dot_general(
        left, right, (((1,), (1,)), ((), ())), preferred_element_type=jnp.float32
    )


def layer_kernel(
    layers,
    pieces,
    gate_hbm,
    up_hbm,
    down_hbm,
    key_hbm,
    value_hbm,
    query_hbm,
    side_hbm,
    weight_hbm,
    rate_ref,
    gain_ref,
    out_ref,
    fast,
    fresh,
    keys,
    values,
    rates,
    queries,
    side,
    opened,
    full,
    grads,
    heads,
    mixed,
    normed,
    laid,
    local_sem,
    ctx_send,
    ctx_recv,
    full_send,
    full_recv,
    head_send,
    head_recv,
    fresh_send,
    fresh_recv,
):
    ctx = lax.axis_index("ctx")
    me = lax.axis_index("hs")
    other = 1 - ctx
    count = 4 * layers
    depth, inner = me // 4, me % 4
    row, core = inner // 2, inner % 2
    row_peer = depth * 4 + (1 - row) * 2 + core
    core_peer = depth * 4 + row * 2 + (1 - core)
    pair = depth * 4 + row * 2 + ctx
    owner = core == ctx
    helper = core != ctx

    def remote(source, target, send, recv, device):
        return pltpu.make_async_remote_copy(
            src_ref=source,
            dst_ref=target,
            send_sem=send,
            recv_sem=recv,
            device_id=device,
            device_id_type=MESH,
        )

    part = gate_hbm.shape[1]
    tokens = key_hbm.shape[1]
    piece = tokens // pieces
    shard = weight_hbm.shape[0]

    def rows(start, size):
        return pl.ds(pl.multiple_of(start, size), size)

    weights = (gate_hbm, up_hbm, down_hbm)
    local = []
    for i, source in enumerate(weights):
        local.append(
            pltpu.make_async_copy(source.at[0], fast.at[i, rows(ctx * part, part)], local_sem.at[i])
        )
    local.append(
        pltpu.make_async_copy(key_hbm.at[0], keys.at[rows(ctx * tokens, tokens)], local_sem.at[3])
    )
    local.append(
        pltpu.make_async_copy(value_hbm.at[0], values.at[rows(ctx * tokens, tokens)], local_sem.at[4])
    )
    local.append(pltpu.make_async_copy(weight_hbm, full.at[rows(me * shard, shard)], local_sem.at[5]))
    local.append(pltpu.make_async_copy(query_hbm.at[0], queries, local_sem.at[6]))
    local.append(pltpu.make_async_copy(side_hbm, side, local_sem.at[7]))
    owned = [0, 1, 2, 3, 4, 6]
    for i in (5, 7):
        local[i].start()

    @pl.when(owner)
    def _():
        for i in owned:
            local[i].start()

    barrier = pltpu.get_barrier_semaphore()
    pl.semaphore_signal(barrier, inc=1, device_id={"ctx": other}, device_id_type=MESH)
    for step in range(1, count):
        for side_ctx in (ctx, other):
            pl.semaphore_signal(
                barrier,
                inc=1,
                device_id={"ctx": side_ctx, "hs": (me + step) % count},
                device_id_type=MESH,
            )
    pl.semaphore_wait(barrier, 2 * count - 1)

    swaps = []
    for i, source in enumerate(weights):
        swaps.append((source.at[0], lambda who, i=i: fast.at[i, rows(who * part, part)]))
    for j in range(pieces):
        for source, target in ((key_hbm.at[0], keys), (value_hbm.at[0], values)):
            swaps.append(
                (
                    source.at[pl.ds(j * piece, piece)],
                    lambda who, target=target, j=j: target.at[
                        rows(who * tokens + j * piece, piece)
                    ],
                )
            )
    swaps.append((rate_ref, lambda who: rates))
    outgoing = [
        remote(source, target(ctx), ctx_send.at[i], ctx_recv.at[i], {"ctx": other})
        for i, (source, target) in enumerate(swaps)
    ]
    incoming = [
        remote(source, target(other), ctx_send.at[i], ctx_recv.at[i], {"ctx": other})
        for i, (source, target) in enumerate(swaps)
    ]
    asked = remote(
        query_hbm.at[0],
        queries,
        ctx_send.at[len(swaps)],
        ctx_recv.at[len(swaps)],
        {"ctx": other, "hs": core_peer},
    )

    @pl.when(helper)
    def _():
        for copy in outgoing[-1:] + outgoing[:-1]:
            copy.start()
        asked.start()

    def full_copy(source, index, slot, device):
        return remote(
            source,
            full.at[rows(index * shard, shard)],
            full_send.at[slot],
            full_recv.at[index],
            {"hs": device},
        )

    def arrived(index):
        block = full.at[rows(index * shard, shard)]
        remote(block, block, full_send.at[0], full_recv.at[index], {"hs": core_peer}).wait_recv()

    def held(index):
        return full.at[rows(index * shard, shard)]

    sends = [
        (depth < layers - 1, full_copy(weight_hbm, me, 0, me + 4)),
        (depth > 0, full_copy(weight_hbm, me, 1, me - 4)),
        (None, full_copy(weight_hbm, me, 2, row_peer)),
        (None, full_copy(weight_hbm, me, 3, core_peer)),
    ]

    def guarded(condition, action):
        if condition is None:
            action()
        else:
            pl.when(condition)(action)

    for condition, copy in sends:
        guarded(condition, copy.start)

    def relay(hop):
        for turn, (exists, onward) in enumerate(
            (
                (depth >= hop, depth < layers - 1),
                (depth + hop <= layers - 1, depth > 0),
            )
        ):
            index = me - 4 * hop if turn == 0 else me + 4 * hop
            slot = 4 + ((hop - 1) * 2 + turn) * 3
            next_device = me + 4 if turn == 0 else me - 4
            made = [
                (exists & onward, full_copy(held(index), index, slot, next_device)),
                (exists, full_copy(held(index), index, slot + 1, row_peer)),
                (exists, full_copy(held(index), index, slot + 2, core_peer)),
            ]
            pl.when(exists)(functools.partial(arrived, index))
            for condition, copy in made:
                guarded(condition, copy.start)
            sends.extend(made)

    crossed = []
    for step in range(layers):
        index = ((depth + step) % layers) * 4 + (1 - row) * 2 + core
        slot = 4 + 6 * (layers - 1) + step
        crossed.append((index, full_copy(held(index), index, slot, core_peer)))

    def cross():
        for index, copy in crossed:
            arrived(index)
            copy.start()

    def learn(start, rate, first):
        key_part = keys[rows(start, piece), :]
        rate_column = jnp.broadcast_to(rate, (128, piece)).T[:, :1]
        scaled_part = (rate_column * values[rows(start, piece), :].astype(jnp.float32)).astype(
            jnp.bfloat16
        )
        pre_gate = inner_cols(key_part, fast[0])
        pre_up = inner_cols(key_part, fast[1])
        sig_gate = jax.nn.sigmoid(pre_gate)
        act_gate = pre_gate * sig_gate
        hidden = (act_gate * pre_up).astype(jnp.bfloat16)
        back_hidden = jnp.dot(scaled_part, fast[2], preferred_element_type=jnp.float32)
        back_gate = (
            back_hidden * pre_up * sig_gate * (1.0 + pre_gate * (1.0 - sig_gate))
        ).astype(jnp.bfloat16)
        back_up = (back_hidden * act_gate).astype(jnp.bfloat16)
        terms = (
            inner_rows(back_gate, key_part),
            inner_rows(back_up, key_part),
            inner_rows(scaled_part, hidden),
        )
        for i, term in enumerate(terms):
            grads[i] = term if first else grads[i] + term

    handed = [
        remote(fresh.at[i], fresh.at[i], fresh_send.at[i], fresh_recv.at[i], {"hs": core_peer})
        for i in range(3)
    ]
    local[7].wait()
    gate = side[...].astype(jnp.float32)
    opened[...] = gate * jax.nn.sigmoid(gate)
    hops = list(range(1, layers))
    if hops:
        relay(hops.pop(0))

    @pl.when(owner)
    def _():
        for i in owned[:5]:
            local[i].wait()
        for copy in incoming[:3]:
            copy.wait_recv()
        for j in range(pieces):
            learn(ctx * tokens + j * piece, rate_ref[:, j * piece : (j + 1) * piece], j == 0)

    for j in range(pieces):
        if hops:
            relay(hops.pop(0))

        @pl.when(owner)
        def _():
            if j == 0:
                incoming[-1].wait_recv()
            incoming[3 + 2 * j].wait_recv()
            incoming[4 + 2 * j].wait_recv()
            learn(other * tokens + j * piece, rates[:, j * piece : (j + 1) * piece], False)

    for hop in hops:
        relay(hop)

    @pl.when(owner)
    def _():
        for i in range(3):
            fresh[i] = rescale_rows(fast[i], grads[i])
            handed[i].start()
        local[6].wait()

    @pl.when(helper)
    def _():
        cross()
        asked.wait_recv()
        for copy in handed:
            copy.wait_recv()

    block_rows = tokens // count
    step_rows = 4 * block_rows
    copies = []
    for step in range(1, layers + 1):
        target = (depth + step) % layers
        query_part = queries[rows(target * step_rows, step_rows), :]
        query_gate = inner_cols(query_part, fresh[0])
        query_up = inner_cols(query_part, fresh[1])
        query_hidden = (query_gate * jax.nn.sigmoid(query_gate) * query_up).astype(jnp.bfloat16)
        head_part = inner_cols(query_hidden, fresh[2]).astype(jnp.bfloat16)
        heads[rows(target * step_rows, step_rows), :] = head_part
        for i in range(4):
            device = target * 4 + (inner + i) % 4
            source = heads.at[rows(device * block_rows, block_rows)]
            slot = len(copies)
            copy = remote(
                source,
                mixed.at[pair],
                head_send.at[slot],
                head_recv.at[pair],
                {"ctx": core, "hs": device},
            )
            condition = None
            if step == layers and i == 0:
                condition = helper

                @pl.when(owner)
                def _():
                    mixed[me] = source[...]

            guarded(condition, copy.start)
            copies.append((condition, copy))

    pl.when(owner)(cross)
    local[5].wait()
    for step in range(layers):
        for other_row in range(2):
            arrived(((depth + step) % layers) * 4 + ((row + other_row) % 2) * 2 + (1 - core))

    def head_arrived(index):
        remote(
            heads.at[pl.ds(0, block_rows)],
            mixed.at[index],
            head_send.at[0],
            head_recv.at[index],
            {"hs": core_peer},
        ).wait_recv()

    for step in range(1, count):
        head_arrived((me + step) % count)
    pl.when(helper)(functools.partial(head_arrived, me))

    for condition, copy in sends + copies:
        guarded(condition, copy.wait_send)
    for _, copy in crossed:
        copy.wait_send()

    @pl.when(helper)
    def _():
        for copy in outgoing:
            copy.wait_send()
        asked.wait_send()

    @pl.when(owner)
    def _():
        for copy in handed:
            copy.wait_send()

    size = mixed.shape[2]
    head_count = side.shape[2] // size
    for seq in range(side.shape[1]):
        for head in range(head_count):
            columns = slice(head * size, (head + 1) * size)
            value = mixed[seq * head_count + head].astype(jnp.float32)
            square = jnp.mean(value * value, -1, keepdims=True)
            value = value * lax.rsqrt(square + epsilon) * gain_ref[:, columns]
            normed[seq * block_rows : (seq + 1) * block_rows, columns] = (
                value * opened[:, seq, columns]
            ).astype(jnp.bfloat16)
    result = jnp.dot(normed[...], full[...], preferred_element_type=jnp.float32)
    for seq in range(side.shape[1]):
        laid[:, seq, :] = result[seq * block_rows : (seq + 1) * block_rows]
    out_ref[...] = laid[...].astype(jnp.bfloat16)


def swapped_body(
    key_rows,
    value_rows,
    query_rows,
    step_rates,
    fast_gate,
    fast_up,
    fast_down,
    out_gain,
    gate_input,
    out_weight,
):
    layers = lax.axis_size("hs") // 4
    count = 4 * layers
    pieces = 2
    tokens, size = key_rows.shape[1:]
    hidden_size = 2 * fast_gate.shape[1]
    block_rows, seq_count, width = gate_input.shape
    columns = out_weight.shape[1]
    anywhere = pl.BlockSpec(memory_space=pl.ANY)
    inside = pl.BlockSpec(memory_space=pltpu.VMEM)
    half = jnp.bfloat16
    return pl.pallas_call(
        functools.partial(layer_kernel, layers, pieces),
        out_shape=jax.ShapeDtypeStruct((block_rows, seq_count, columns), half),
        in_specs=[anywhere] * 8 + [inside] * 2,
        out_specs=inside,
        scratch_shapes=[
            pltpu.VMEM((3, hidden_size, size), half),
            pltpu.VMEM((3, hidden_size, size), half),
            pltpu.VMEM((2 * tokens, size), half),
            pltpu.VMEM((2 * tokens, size), half),
            pltpu.VMEM((1, tokens), jnp.float32),
            pltpu.VMEM((tokens, size), half),
            pltpu.VMEM((block_rows, seq_count, width), half),
            pltpu.VMEM((block_rows, seq_count, width), jnp.float32),
            pltpu.VMEM((width, columns), half),
            pltpu.VMEM((3, hidden_size, size), jnp.float32),
            pltpu.VMEM((tokens, size), half),
            pltpu.VMEM((count, block_rows, size), half),
            pltpu.VMEM((seq_count * block_rows, width), half),
            pltpu.VMEM((block_rows, seq_count, columns), jnp.float32),
            pltpu.SemaphoreType.DMA((8,)),
            pltpu.SemaphoreType.DMA((5 + 2 * pieces,)),
            pltpu.SemaphoreType.DMA((5 + 2 * pieces,)),
            pltpu.SemaphoreType.DMA((4 + 6 * (layers - 1) + layers,)),
            pltpu.SemaphoreType.DMA((count,)),
            pltpu.SemaphoreType.DMA((count,)),
            pltpu.SemaphoreType.DMA((count,)),
            pltpu.SemaphoreType.DMA((3,)),
            pltpu.SemaphoreType.DMA((3,)),
        ],
        compiler_params=pltpu.CompilerParams(
            collective_id=0, has_side_effects=True, vmem_limit_bytes=60 * 1024 * 1024
        ),
    )(
        fast_gate,
        fast_up,
        fast_down,
        key_rows,
        value_rows,
        query_rows,
        gate_input,
        out_weight,
        step_rates,
        out_gain[None],
    )

def solution(mesh):
    def step(*arrays):
        paired = mesh.shape["ctx"] == 2 and mesh.shape["hs"] % 4 == 0
        paired = paired and arrays[0].shape[0] == 1
        return (swapped_body if paired else body)(*arrays)

    return jax.shard_map(
        step,
        mesh=mesh,
        in_specs=(
            P("hs", "ctx", None),
            P("hs", "ctx", None),
            P("hs", "ctx", None),
            P("hs", "ctx"),
            P("hs", "ctx", None),
            P("hs", "ctx", None),
            P("hs", "ctx", None),
            P(),
            P(("ctx", "hs"), None, None),
            P("hs", None),
        ),
        out_specs=P(("ctx", "hs"), None, None),
        check_vma=False,
    )
```

```python
import functools

import jax
import jax.numpy as jnp
from jax import lax
from jax.experimental import pallas as pl
from jax.experimental.pallas import tpu as pltpu
from jax.sharding import PartitionSpec as P

epsilon = 1e-06


def rescale_rows(weight, update):
    base = weight.astype(jnp.float32)
    moved = base + update
    factor = jnp.sqrt(jnp.mean(base * base, -1, keepdims=True) + epsilon) / jnp.sqrt(
        jnp.mean(moved * moved, -1, keepdims=True) + epsilon
    )
    return (moved * factor).astype(jnp.bfloat16)


def inner_rows(left, right):
    return lax.dot_general(
        left, right, (((0,), (0,)), ((), ())), preferred_element_type=jnp.float32
    )


def body(
    key_rows,
    value_rows,
    query_rows,
    step_rates,
    fast_gate,
    fast_up,
    fast_down,
    out_gain,
    gate_input,
    out_weight,
):
    key_row = key_rows[0]
    value_row = value_rows[0]
    query_row = query_rows[0]
    rate_row = step_rates[0]
    whole_gate, whole_up, whole_down = (
        lax.all_gather(fast_gate, "ctx", axis=1, tiled=True),
        lax.all_gather(fast_up, "ctx", axis=1, tiled=True),
        lax.all_gather(fast_down, "ctx", axis=1, tiled=True),
    )
    gate_fast = whole_gate[0]
    up_fast = whole_up[0]
    down_fast = whole_down[0]
    pre_gate = jnp.dot(key_row, gate_fast.T, preferred_element_type=jnp.float32)
    pre_up = jnp.dot(key_row, up_fast.T, preferred_element_type=jnp.float32)
    sig_gate = jax.nn.sigmoid(pre_gate)
    act_gate = pre_gate * sig_gate
    hidden = (act_gate * pre_up).astype(jnp.bfloat16)
    scaled = (rate_row[:, None] * value_row.astype(jnp.float32)).astype(jnp.bfloat16)
    grad_down = inner_rows(scaled, hidden)
    back_hidden = jnp.dot(scaled, down_fast, preferred_element_type=jnp.float32)
    back_gate = (back_hidden * pre_up * sig_gate * (1.0 + pre_gate * (1.0 - sig_gate))).astype(
        jnp.bfloat16
    )
    back_up = (back_hidden * act_gate).astype(jnp.bfloat16)
    grad_gate = inner_rows(back_gate, key_row)
    grad_up = inner_rows(back_up, key_row)
    grad_gate, grad_up, grad_down = (
        lax.psum_scatter(grad_gate, "ctx", scatter_dimension=0, tiled=True),
        lax.psum_scatter(grad_up, "ctx", scatter_dimension=0, tiled=True),
        lax.psum_scatter(grad_down, "ctx", scatter_dimension=0, tiled=True),
    )
    part_gate = rescale_rows(fast_gate[0], grad_gate)
    part_up = rescale_rows(fast_up[0], grad_up)
    part_down = rescale_rows(fast_down[0], grad_down)
    new_gate, new_up, new_down = (
        lax.all_gather(part_gate, "ctx", axis=0, tiled=True),
        lax.all_gather(part_up, "ctx", axis=0, tiled=True),
        lax.all_gather(part_down, "ctx", axis=0, tiled=True),
    )
    query_gate = jnp.dot(query_row, new_gate.T, preferred_element_type=jnp.float32)
    query_up = jnp.dot(query_row, new_up.T, preferred_element_type=jnp.float32)
    query_hidden = (jax.nn.silu(query_gate) * query_up).astype(jnp.bfloat16)
    head_out = jnp.dot(query_hidden, new_down.T, preferred_element_type=jnp.float32).astype(
        jnp.bfloat16
    )
    width_hs = lax.axis_size("hs")
    head_size = head_out.shape[1]
    token_count = head_out.shape[0] // width_hs
    blocks = head_out.reshape(width_hs, token_count, head_size)
    moved = lax.all_to_all(blocks, "hs", split_axis=0, concat_axis=2, tiled=True)
    seq_count = gate_input.shape[1]
    model_width = gate_input.shape[2]
    head_count = model_width // head_size
    mixed = moved.reshape(token_count, seq_count, head_count, head_size).astype(jnp.float32)
    square = jnp.mean(mixed * mixed, -1, keepdims=True)
    scaled_heads = mixed * lax.rsqrt(square + epsilon) * out_gain.reshape(head_count, head_size)
    normed = (
        scaled_heads.reshape(token_count, seq_count, model_width)
        * jax.nn.silu(gate_input.astype(jnp.float32))
    ).astype(jnp.bfloat16)
    flat_rows = normed.reshape(token_count * seq_count, model_width)
    out_cols = out_weight.shape[1]
    full_weight = lax.all_gather(out_weight, "hs", axis=0, tiled=True)
    result = jnp.dot(flat_rows, full_weight, preferred_element_type=jnp.float32)
    return result.astype(jnp.bfloat16).reshape(token_count, seq_count, out_cols)


MESH = pl.DeviceIdType.MESH


def inner_cols(left, right):
    return lax.dot_general(
        left, right, (((1,), (1,)), ((), ())), preferred_element_type=jnp.float32
    )


def layer_kernel(
    layers,
    pieces,
    gate_hbm,
    up_hbm,
    down_hbm,
    key_hbm,
    value_hbm,
    query_hbm,
    side_hbm,
    weight_hbm,
    rate_ref,
    gain_ref,
    out_ref,
    fast,
    fresh,
    keys,
    values,
    rates,
    queries,
    side,
    opened,
    full,
    grads,
    heads,
    mixed,
    normed,
    laid,
    local_sem,
    ctx_send,
    ctx_recv,
    full_send,
    full_recv,
    head_send,
    head_recv,
    fresh_send,
    fresh_recv,
):
    ctx = lax.axis_index("ctx")
    me = lax.axis_index("hs")
    other = 1 - ctx
    count = 4 * layers
    depth, inner = me // 4, me % 4
    row, core = inner // 2, inner % 2
    row_peer = depth * 4 + (1 - row) * 2 + core
    core_peer = depth * 4 + row * 2 + (1 - core)
    pair = depth * 4 + row * 2 + ctx
    owner = core == ctx
    helper = core != ctx

    def remote(source, target, send, recv, device):
        return pltpu.make_async_remote_copy(
            src_ref=source,
            dst_ref=target,
            send_sem=send,
            recv_sem=recv,
            device_id=device,
            device_id_type=MESH,
        )

    part = gate_hbm.shape[1]
    tokens = key_hbm.shape[1]
    piece = tokens // pieces
    shard = weight_hbm.shape[0]

    def rows(start, size):
        return pl.ds(pl.multiple_of(start, size), size)

    weights = (gate_hbm, up_hbm, down_hbm)
    local = []
    for i, source in enumerate(weights):
        local.append(
            pltpu.make_async_copy(source.at[0], fast.at[i, rows(ctx * part, part)], local_sem.at[i])
        )
    local.append(
        pltpu.make_async_copy(key_hbm.at[0], keys.at[rows(ctx * tokens, tokens)], local_sem.at[3])
    )
    local.append(
        pltpu.make_async_copy(value_hbm.at[0], values.at[rows(ctx * tokens, tokens)], local_sem.at[4])
    )
    local.append(pltpu.make_async_copy(weight_hbm, full.at[rows(me * shard, shard)], local_sem.at[5]))
    local.append(pltpu.make_async_copy(query_hbm.at[0], queries, local_sem.at[6]))
    local.append(pltpu.make_async_copy(side_hbm, side, local_sem.at[7]))
    owned = [0, 1, 2, 3, 4, 6]
    for i in (5, 7):
        local[i].start()

    @pl.when(owner)
    def _():
        for i in owned:
            local[i].start()

    barrier = pltpu.get_barrier_semaphore()
    pl.semaphore_signal(barrier, inc=1, device_id={"ctx": other}, device_id_type=MESH)
    for step in range(1, count):
        for side_ctx in (ctx, other):
            pl.semaphore_signal(
                barrier,
                inc=1,
                device_id={"ctx": side_ctx, "hs": (me + step) % count},
                device_id_type=MESH,
            )
    pl.semaphore_wait(barrier, 2 * count - 1)

    swaps = []
    for i, source in enumerate(weights):
        swaps.append((source.at[0], lambda who, i=i: fast.at[i, rows(who * part, part)]))
    for j in range(pieces):
        for source, target in ((key_hbm.at[0], keys), (value_hbm.at[0], values)):
            swaps.append(
                (
                    source.at[pl.ds(j * piece, piece)],
                    lambda who, target=target, j=j: target.at[
                        rows(who * tokens + j * piece, piece)
                    ],
                )
            )
    swaps.append((rate_ref, lambda who: rates))
    outgoing = [
        remote(source, target(ctx), ctx_send.at[i], ctx_recv.at[i], {"ctx": other})
        for i, (source, target) in enumerate(swaps)
    ]
    incoming = [
        remote(source, target(other), ctx_send.at[i], ctx_recv.at[i], {"ctx": other})
        for i, (source, target) in enumerate(swaps)
    ]
    block_rows = tokens // count
    step_rows = 4 * block_rows
    asked = []
    for step in range(layers):
        span = rows(((depth + step + 1) % layers) * step_rows, step_rows)
        slot = len(swaps) + step
        asked.append(
            remote(
                query_hbm.at[0, span],
                queries.at[span],
                ctx_send.at[slot],
                ctx_recv.at[slot],
                {"ctx": other, "hs": core_peer},
            )
        )

    @pl.when(helper)
    def _():
        for copy in outgoing[-1:] + outgoing[:-1] + asked:
            copy.start()

    def full_copy(source, index, slot, device):
        return remote(
            source,
            full.at[rows(index * shard, shard)],
            full_send.at[slot],
            full_recv.at[index],
            {"hs": device},
        )

    def arrived(index):
        block = full.at[rows(index * shard, shard)]
        remote(block, block, full_send.at[0], full_recv.at[index], {"hs": core_peer}).wait_recv()

    def held(index):
        return full.at[rows(index * shard, shard)]

    sends = [
        (depth < layers - 1, full_copy(weight_hbm, me, 0, me + 4)),
        (depth > 0, full_copy(weight_hbm, me, 1, me - 4)),
        (None, full_copy(weight_hbm, me, 2, row_peer)),
        (None, full_copy(weight_hbm, me, 3, core_peer)),
    ]

    def guarded(condition, action):
        if condition is None:
            action()
        else:
            pl.when(condition)(action)

    for condition, copy in sends:
        guarded(condition, copy.start)

    def relay(hop):
        for turn, (exists, onward) in enumerate(
            (
                (depth >= hop, depth < layers - 1),
                (depth + hop <= layers - 1, depth > 0),
            )
        ):
            index = me - 4 * hop if turn == 0 else me + 4 * hop
            slot = 4 + ((hop - 1) * 2 + turn) * 3
            next_device = me + 4 if turn == 0 else me - 4
            made = [
                (exists & onward, full_copy(held(index), index, slot, next_device)),
                (exists, full_copy(held(index), index, slot + 1, row_peer)),
                (exists, full_copy(held(index), index, slot + 2, core_peer)),
            ]
            pl.when(exists)(functools.partial(arrived, index))
            for condition, copy in made:
                guarded(condition, copy.start)
            sends.extend(made)

    crossed = []
    for step in range(layers):
        index = ((depth + step) % layers) * 4 + (1 - row) * 2 + core
        slot = 4 + 6 * (layers - 1) + step
        crossed.append((index, full_copy(held(index), index, slot, core_peer)))

    def cross():
        for index, copy in crossed:
            arrived(index)
            copy.start()

    def learn(start, rate, first):
        key_part = keys[rows(start, piece), :]
        rate_column = jnp.broadcast_to(rate, (128, piece)).T[:, :1]
        scaled_part = (rate_column * values[rows(start, piece), :].astype(jnp.float32)).astype(
            jnp.bfloat16
        )
        pre_gate = inner_cols(key_part, fast[0])
        pre_up = inner_cols(key_part, fast[1])
        sig_gate = jax.nn.sigmoid(pre_gate)
        act_gate = pre_gate * sig_gate
        hidden = (act_gate * pre_up).astype(jnp.bfloat16)
        back_hidden = jnp.dot(scaled_part, fast[2], preferred_element_type=jnp.float32)
        back_gate = (
            back_hidden * pre_up * sig_gate * (1.0 + pre_gate * (1.0 - sig_gate))
        ).astype(jnp.bfloat16)
        back_up = (back_hidden * act_gate).astype(jnp.bfloat16)
        terms = (
            inner_rows(back_gate, key_part),
            inner_rows(back_up, key_part),
            inner_rows(scaled_part, hidden),
        )
        for i, term in enumerate(terms):
            grads[i] = term if first else grads[i] + term

    handed = [
        remote(fresh.at[i], fresh.at[i], fresh_send.at[i], fresh_recv.at[i], {"hs": core_peer})
        for i in range(3)
    ]
    local[7].wait()
    gate = side[...].astype(jnp.float32)
    opened[...] = gate * jax.nn.sigmoid(gate)
    hops = list(range(1, layers))
    if hops:
        relay(hops.pop(0))

    @pl.when(owner)
    def _():
        for i in owned[:5]:
            local[i].wait()
        for copy in incoming[:3]:
            copy.wait_recv()
        for j in range(pieces):
            learn(ctx * tokens + j * piece, rate_ref[:, j * piece : (j + 1) * piece], j == 0)

    for j in range(pieces):
        if hops:
            relay(hops.pop(0))

        @pl.when(owner)
        def _():
            if j == 0:
                incoming[-1].wait_recv()
            incoming[3 + 2 * j].wait_recv()
            incoming[4 + 2 * j].wait_recv()
            learn(other * tokens + j * piece, rates[:, j * piece : (j + 1) * piece], False)

    for hop in hops:
        relay(hop)

    @pl.when(owner)
    def _():
        for i in range(3):
            fresh[i] = rescale_rows(fast[i], grads[i])
            handed[i].start()
        local[6].wait()

    @pl.when(helper)
    def _():
        cross()
        for copy in handed:
            copy.wait_recv()

    copies = []
    for step in range(1, layers + 1):
        target = (depth + step) % layers
        pl.when(helper)(asked[step - 1].wait_recv)
        query_part = queries[rows(target * step_rows, step_rows), :]
        query_gate = inner_cols(query_part, fresh[0])
        query_up = inner_cols(query_part, fresh[1])
        query_hidden = (query_gate * jax.nn.sigmoid(query_gate) * query_up).astype(jnp.bfloat16)
        head_part = inner_cols(query_hidden, fresh[2]).astype(jnp.bfloat16)
        heads[rows(target * step_rows, step_rows), :] = head_part
        for i in range(4):
            device = target * 4 + (inner + i) % 4
            source = heads.at[rows(device * block_rows, block_rows)]
            slot = len(copies)
            copy = remote(
                source,
                mixed.at[pair],
                head_send.at[slot],
                head_recv.at[pair],
                {"ctx": core, "hs": device},
            )
            condition = None
            if step == layers and i == 0:
                condition = helper

                @pl.when(owner)
                def _():
                    mixed[me] = source[...]

            guarded(condition, copy.start)
            copies.append((condition, copy))

    pl.when(owner)(cross)
    local[5].wait()
    for step in range(layers):
        for other_row in range(2):
            arrived(((depth + step) % layers) * 4 + ((row + other_row) % 2) * 2 + (1 - core))

    def head_arrived(index):
        remote(
            heads.at[pl.ds(0, block_rows)],
            mixed.at[index],
            head_send.at[0],
            head_recv.at[index],
            {"hs": core_peer},
        ).wait_recv()

    size = mixed.shape[2]
    head_count = side.shape[2] // size
    seqs = side.shape[1]
    result = None
    for late in range(2):
        for half in range(head_count // 2):
            head = 2 * half + (other if late else ctx)
            columns = rows(head * size, size)
            for seq in range(seqs):
                index = seq * head_count + head
                guarded(None if late else index != me, functools.partial(head_arrived, index))
                value = mixed[index].astype(jnp.float32)
                square = jnp.mean(value * value, -1, keepdims=True)
                value = value * lax.rsqrt(square + epsilon) * gain_ref[:, columns]
                normed[seq * block_rows : (seq + 1) * block_rows, columns] = (
                    value * opened[:, seq, columns]
                ).astype(jnp.bfloat16)
            term = jnp.dot(
                normed[:, columns], full[columns, :], preferred_element_type=jnp.float32
            )
            result = term if result is None else result + term

    for seq in range(side.shape[1]):
        laid[:, seq, :] = result[seq * block_rows : (seq + 1) * block_rows]
    out_ref[...] = laid[...].astype(jnp.bfloat16)
    for condition, copy in sends + copies:
        guarded(condition, copy.wait_send)
    for _, copy in crossed:
        copy.wait_send()

    @pl.when(helper)
    def _():
        for copy in outgoing + asked:
            copy.wait_send()

    @pl.when(owner)
    def _():
        for copy in handed:
            copy.wait_send()


def swapped_body(
    key_rows,
    value_rows,
    query_rows,
    step_rates,
    fast_gate,
    fast_up,
    fast_down,
    out_gain,
    gate_input,
    out_weight,
):
    layers = lax.axis_size("hs") // 4
    count = 4 * layers
    pieces = 2
    tokens, size = key_rows.shape[1:]
    hidden_size = 2 * fast_gate.shape[1]
    block_rows, seq_count, width = gate_input.shape
    columns = out_weight.shape[1]
    anywhere = pl.BlockSpec(memory_space=pl.ANY)
    inside = pl.BlockSpec(memory_space=pltpu.VMEM)
    half = jnp.bfloat16
    return pl.pallas_call(
        functools.partial(layer_kernel, layers, pieces),
        out_shape=jax.ShapeDtypeStruct((block_rows, seq_count, columns), half),
        in_specs=[anywhere] * 8 + [inside] * 2,
        out_specs=inside,
        scratch_shapes=[
            pltpu.VMEM((3, hidden_size, size), half),
            pltpu.VMEM((3, hidden_size, size), half),
            pltpu.VMEM((2 * tokens, size), half),
            pltpu.VMEM((2 * tokens, size), half),
            pltpu.VMEM((1, tokens), jnp.float32),
            pltpu.VMEM((tokens, size), half),
            pltpu.VMEM((block_rows, seq_count, width), half),
            pltpu.VMEM((block_rows, seq_count, width), jnp.float32),
            pltpu.VMEM((width, columns), half),
            pltpu.VMEM((3, hidden_size, size), jnp.float32),
            pltpu.VMEM((tokens, size), half),
            pltpu.VMEM((count, block_rows, size), half),
            pltpu.VMEM((seq_count * block_rows, width), half),
            pltpu.VMEM((block_rows, seq_count, columns), jnp.float32),
            pltpu.SemaphoreType.DMA((8,)),
            pltpu.SemaphoreType.DMA((4 + 2 * pieces + layers,)),
            pltpu.SemaphoreType.DMA((4 + 2 * pieces + layers,)),
            pltpu.SemaphoreType.DMA((4 + 6 * (layers - 1) + layers,)),
            pltpu.SemaphoreType.DMA((count,)),
            pltpu.SemaphoreType.DMA((count,)),
            pltpu.SemaphoreType.DMA((count,)),
            pltpu.SemaphoreType.DMA((3,)),
            pltpu.SemaphoreType.DMA((3,)),
        ],
        compiler_params=pltpu.CompilerParams(
            collective_id=0, has_side_effects=True, vmem_limit_bytes=60 * 1024 * 1024
        ),
    )(
        fast_gate,
        fast_up,
        fast_down,
        key_rows,
        value_rows,
        query_rows,
        gate_input,
        out_weight,
        step_rates,
        out_gain[None],
    )

def solution(mesh):
    def step(*arrays):
        paired = mesh.shape["ctx"] == 2 and mesh.shape["hs"] % 4 == 0
        paired = paired and arrays[8].shape[2] // arrays[0].shape[2] % 2 == 0
        paired = paired and arrays[0].shape[0] == 1
        return (swapped_body if paired else body)(*arrays)

    return jax.shard_map(
        step,
        mesh=mesh,
        in_specs=(
            P("hs", "ctx", None),
            P("hs", "ctx", None),
            P("hs", "ctx", None),
            P("hs", "ctx"),
            P("hs", "ctx", None),
            P("hs", "ctx", None),
            P("hs", "ctx", None),
            P(),
            P(("ctx", "hs"), None, None),
            P("hs", None),
        ),
        out_specs=P(("ctx", "hs"), None, None),
        check_vma=False,
    )
```

```python
import functools

import jax
import jax.numpy as jnp
from jax import lax
from jax.experimental import pallas as pl
from jax.experimental.pallas import tpu as pltpu
from jax.sharding import PartitionSpec as P

epsilon = 1e-06


def rescale_rows(weight, update):
    base = weight.astype(jnp.float32)
    moved = base + update
    factor = jnp.sqrt(jnp.mean(base * base, -1, keepdims=True) + epsilon) / jnp.sqrt(
        jnp.mean(moved * moved, -1, keepdims=True) + epsilon
    )
    return (moved * factor).astype(jnp.bfloat16)


def inner_rows(left, right):
    return lax.dot_general(
        left, right, (((0,), (0,)), ((), ())), preferred_element_type=jnp.float32
    )


def body(
    key_rows,
    value_rows,
    query_rows,
    step_rates,
    fast_gate,
    fast_up,
    fast_down,
    out_gain,
    gate_input,
    out_weight,
):
    key_row = key_rows[0]
    value_row = value_rows[0]
    query_row = query_rows[0]
    rate_row = step_rates[0]
    whole_gate, whole_up, whole_down = (
        lax.all_gather(fast_gate, "ctx", axis=1, tiled=True),
        lax.all_gather(fast_up, "ctx", axis=1, tiled=True),
        lax.all_gather(fast_down, "ctx", axis=1, tiled=True),
    )
    gate_fast = whole_gate[0]
    up_fast = whole_up[0]
    down_fast = whole_down[0]
    pre_gate = jnp.dot(key_row, gate_fast.T, preferred_element_type=jnp.float32)
    pre_up = jnp.dot(key_row, up_fast.T, preferred_element_type=jnp.float32)
    sig_gate = jax.nn.sigmoid(pre_gate)
    act_gate = pre_gate * sig_gate
    hidden = (act_gate * pre_up).astype(jnp.bfloat16)
    scaled = (rate_row[:, None] * value_row.astype(jnp.float32)).astype(jnp.bfloat16)
    grad_down = inner_rows(scaled, hidden)
    back_hidden = jnp.dot(scaled, down_fast, preferred_element_type=jnp.float32)
    back_gate = (back_hidden * pre_up * sig_gate * (1.0 + pre_gate * (1.0 - sig_gate))).astype(
        jnp.bfloat16
    )
    back_up = (back_hidden * act_gate).astype(jnp.bfloat16)
    grad_gate = inner_rows(back_gate, key_row)
    grad_up = inner_rows(back_up, key_row)
    grad_gate, grad_up, grad_down = (
        lax.psum_scatter(grad_gate, "ctx", scatter_dimension=0, tiled=True),
        lax.psum_scatter(grad_up, "ctx", scatter_dimension=0, tiled=True),
        lax.psum_scatter(grad_down, "ctx", scatter_dimension=0, tiled=True),
    )
    part_gate = rescale_rows(fast_gate[0], grad_gate)
    part_up = rescale_rows(fast_up[0], grad_up)
    part_down = rescale_rows(fast_down[0], grad_down)
    new_gate, new_up, new_down = (
        lax.all_gather(part_gate, "ctx", axis=0, tiled=True),
        lax.all_gather(part_up, "ctx", axis=0, tiled=True),
        lax.all_gather(part_down, "ctx", axis=0, tiled=True),
    )
    query_gate = jnp.dot(query_row, new_gate.T, preferred_element_type=jnp.float32)
    query_up = jnp.dot(query_row, new_up.T, preferred_element_type=jnp.float32)
    query_hidden = (jax.nn.silu(query_gate) * query_up).astype(jnp.bfloat16)
    head_out = jnp.dot(query_hidden, new_down.T, preferred_element_type=jnp.float32).astype(
        jnp.bfloat16
    )
    width_hs = lax.axis_size("hs")
    head_size = head_out.shape[1]
    token_count = head_out.shape[0] // width_hs
    blocks = head_out.reshape(width_hs, token_count, head_size)
    moved = lax.all_to_all(blocks, "hs", split_axis=0, concat_axis=2, tiled=True)
    seq_count = gate_input.shape[1]
    model_width = gate_input.shape[2]
    head_count = model_width // head_size
    mixed = moved.reshape(token_count, seq_count, head_count, head_size).astype(jnp.float32)
    square = jnp.mean(mixed * mixed, -1, keepdims=True)
    scaled_heads = mixed * lax.rsqrt(square + epsilon) * out_gain.reshape(head_count, head_size)
    normed = (
        scaled_heads.reshape(token_count, seq_count, model_width)
        * jax.nn.silu(gate_input.astype(jnp.float32))
    ).astype(jnp.bfloat16)
    flat_rows = normed.reshape(token_count * seq_count, model_width)
    out_cols = out_weight.shape[1]
    full_weight = lax.all_gather(out_weight, "hs", axis=0, tiled=True)
    result = jnp.dot(flat_rows, full_weight, preferred_element_type=jnp.float32)
    return result.astype(jnp.bfloat16).reshape(token_count, seq_count, out_cols)


MESH = pl.DeviceIdType.MESH


def inner_cols(left, right):
    return lax.dot_general(
        left, right, (((1,), (1,)), ((), ())), preferred_element_type=jnp.float32
    )


def layer_kernel(
    layers,
    pieces,
    gate_hbm,
    up_hbm,
    down_hbm,
    key_hbm,
    value_hbm,
    query_hbm,
    side_hbm,
    weight_hbm,
    rate_ref,
    gain_ref,
    out_ref,
    fast,
    fresh,
    keys,
    values,
    rates,
    queries,
    side,
    opened,
    full,
    grads,
    heads,
    mixed,
    normed,
    laid,
    local_sem,
    ctx_send,
    ctx_recv,
    full_send,
    full_recv,
    head_send,
    head_recv,
    fresh_send,
    fresh_recv,
):
    ctx = lax.axis_index("ctx")
    me = lax.axis_index("hs")
    other = 1 - ctx
    count = 4 * layers
    depth, inner = me // 4, me % 4
    row, core = inner // 2, inner % 2
    row_peer = depth * 4 + (1 - row) * 2 + core
    core_peer = depth * 4 + row * 2 + (1 - core)
    pair = depth * 4 + row * 2 + ctx
    owner = core == ctx
    helper = core != ctx

    def remote(source, target, send, recv, device):
        return pltpu.make_async_remote_copy(
            src_ref=source,
            dst_ref=target,
            send_sem=send,
            recv_sem=recv,
            device_id=device,
            device_id_type=MESH,
        )

    part = gate_hbm.shape[1]
    tokens = key_hbm.shape[1]
    piece = tokens // pieces
    shard = weight_hbm.shape[0]

    def rows(start, size):
        return pl.ds(pl.multiple_of(start, size), size)

    weights = (gate_hbm, up_hbm, down_hbm)
    local = []
    for i, source in enumerate(weights):
        local.append(
            pltpu.make_async_copy(source.at[0], fast.at[i, rows(ctx * part, part)], local_sem.at[i])
        )
    local.append(
        pltpu.make_async_copy(key_hbm.at[0], keys.at[rows(ctx * tokens, tokens)], local_sem.at[3])
    )
    local.append(
        pltpu.make_async_copy(value_hbm.at[0], values.at[rows(ctx * tokens, tokens)], local_sem.at[4])
    )
    local.append(pltpu.make_async_copy(weight_hbm, full.at[rows(me * shard, shard)], local_sem.at[5]))
    local.append(pltpu.make_async_copy(query_hbm.at[0], queries, local_sem.at[6]))
    local.append(pltpu.make_async_copy(side_hbm, side, local_sem.at[7]))
    owned = [0, 1, 2, 3, 4, 6]
    for i in (5, 7):
        local[i].start()

    @pl.when(owner)
    def _():
        for i in owned:
            local[i].start()

    barrier = pltpu.get_barrier_semaphore()
    pl.semaphore_signal(barrier, inc=1, device_id={"ctx": other}, device_id_type=MESH)
    for step in range(1, count):
        for side_ctx in (ctx, other):
            pl.semaphore_signal(
                barrier,
                inc=1,
                device_id={"ctx": side_ctx, "hs": (me + step) % count},
                device_id_type=MESH,
            )
    pl.semaphore_wait(barrier, 2 * count - 1)

    swaps = []
    for i, source in enumerate(weights):
        swaps.append((source.at[0], lambda who, i=i: fast.at[i, rows(who * part, part)]))
    for j in range(pieces):
        for source, target in ((key_hbm.at[0], keys), (value_hbm.at[0], values)):
            swaps.append(
                (
                    source.at[pl.ds(j * piece, piece)],
                    lambda who, target=target, j=j: target.at[
                        rows(who * tokens + j * piece, piece)
                    ],
                )
            )
    swaps.append((rate_ref, lambda who: rates))
    outgoing = [
        remote(source, target(ctx), ctx_send.at[i], ctx_recv.at[i], {"ctx": other})
        for i, (source, target) in enumerate(swaps)
    ]
    incoming = [
        remote(source, target(other), ctx_send.at[i], ctx_recv.at[i], {"ctx": other})
        for i, (source, target) in enumerate(swaps)
    ]
    block_rows = tokens // count
    step_rows = 4 * block_rows
    mid = layers // 2
    near = (depth // mid) * mid
    order = [mid - near + (depth + step) % mid for step in range(mid)]
    order += [near + (depth + step) % mid for step in range(1, mid)] + [depth]
    asked = []
    for step in range(layers):
        span = rows(order[step] * step_rows, step_rows)
        slot = len(swaps) + step
        asked.append(
            remote(
                query_hbm.at[0, span],
                queries.at[span],
                ctx_send.at[slot],
                ctx_recv.at[slot],
                {"ctx": other, "hs": core_peer},
            )
        )

    @pl.when(helper)
    def _():
        for copy in outgoing[-1:] + outgoing[:-1] + asked:
            copy.start()

    def full_copy(source, index, slot, device):
        return remote(
            source,
            full.at[rows(index * shard, shard)],
            full_send.at[slot],
            full_recv.at[index],
            {"hs": device},
        )

    def arrived(index):
        block = full.at[rows(index * shard, shard)]
        remote(block, block, full_send.at[0], full_recv.at[index], {"hs": core_peer}).wait_recv()

    def held(index):
        return full.at[rows(index * shard, shard)]

    sends = [
        (depth < layers - 1, full_copy(weight_hbm, me, 0, me + 4)),
        (depth > 0, full_copy(weight_hbm, me, 1, me - 4)),
        (None, full_copy(weight_hbm, me, 2, row_peer)),
        (None, full_copy(weight_hbm, me, 3, core_peer)),
    ]

    def guarded(condition, action):
        if condition is None:
            action()
        else:
            pl.when(condition)(action)

    for condition, copy in sends:
        guarded(condition, copy.start)

    def relay(hop):
        for turn, (exists, onward) in enumerate(
            (
                (depth >= hop, depth < layers - 1),
                (depth + hop <= layers - 1, depth > 0),
            )
        ):
            index = me - 4 * hop if turn == 0 else me + 4 * hop
            slot = 4 + ((hop - 1) * 2 + turn) * 3
            next_device = me + 4 if turn == 0 else me - 4
            made = [
                (exists & onward, full_copy(held(index), index, slot, next_device)),
                (exists, full_copy(held(index), index, slot + 1, row_peer)),
                (exists, full_copy(held(index), index, slot + 2, core_peer)),
            ]
            pl.when(exists)(functools.partial(arrived, index))
            for condition, copy in made:
                guarded(condition, copy.start)
            sends.extend(made)

    crossed = []
    for step in range(layers):
        index = ((depth + step) % layers) * 4 + (1 - row) * 2 + core
        slot = 4 + 6 * (layers - 1) + step
        crossed.append((index, full_copy(held(index), index, slot, core_peer)))

    def cross():
        for index, copy in crossed:
            arrived(index)
            copy.start()

    def learn(start, rate, first):
        key_part = keys[rows(start, piece), :]
        rate_column = jnp.broadcast_to(rate, (128, piece)).T[:, :1]
        scaled_part = (rate_column * values[rows(start, piece), :].astype(jnp.float32)).astype(
            jnp.bfloat16
        )
        pre_gate = inner_cols(key_part, fast[0])
        pre_up = inner_cols(key_part, fast[1])
        sig_gate = jax.nn.sigmoid(pre_gate)
        act_gate = pre_gate * sig_gate
        hidden = (act_gate * pre_up).astype(jnp.bfloat16)
        back_hidden = jnp.dot(scaled_part, fast[2], preferred_element_type=jnp.float32)
        back_gate = (
            back_hidden * pre_up * sig_gate * (1.0 + pre_gate * (1.0 - sig_gate))
        ).astype(jnp.bfloat16)
        back_up = (back_hidden * act_gate).astype(jnp.bfloat16)
        terms = (
            inner_rows(back_gate, key_part),
            inner_rows(back_up, key_part),
            inner_rows(scaled_part, hidden),
        )
        for i, term in enumerate(terms):
            grads[i] = term if first else grads[i] + term

    handed = [
        remote(fresh.at[i], fresh.at[i], fresh_send.at[i], fresh_recv.at[i], {"hs": core_peer})
        for i in range(3)
    ]
    local[7].wait()
    gate = side[...].astype(jnp.float32)
    opened[...] = gate * jax.nn.sigmoid(gate)
    hops = list(range(1, layers))
    if hops:
        relay(hops.pop(0))

    @pl.when(owner)
    def _():
        for i in owned[:5]:
            local[i].wait()
        for copy in incoming[:3]:
            copy.wait_recv()
        for j in range(pieces):
            learn(ctx * tokens + j * piece, rate_ref[:, j * piece : (j + 1) * piece], j == 0)

    for j in range(pieces):
        if hops:
            relay(hops.pop(0))

        @pl.when(owner)
        def _():
            if j == 0:
                incoming[-1].wait_recv()
            incoming[3 + 2 * j].wait_recv()
            incoming[4 + 2 * j].wait_recv()
            learn(other * tokens + j * piece, rates[:, j * piece : (j + 1) * piece], False)

    for hop in hops:
        relay(hop)

    @pl.when(owner)
    def _():
        for i in range(3):
            fresh[i] = rescale_rows(fast[i], grads[i])
            handed[i].start()
        local[6].wait()

    @pl.when(helper)
    def _():
        cross()
        for copy in handed:
            copy.wait_recv()

    copies = []
    for step in range(1, layers + 1):
        target = order[step - 1]
        pl.when(helper)(asked[step - 1].wait_recv)
        query_part = queries[rows(target * step_rows, step_rows), :]
        query_gate = inner_cols(query_part, fresh[0])
        query_up = inner_cols(query_part, fresh[1])
        query_hidden = (query_gate * jax.nn.sigmoid(query_gate) * query_up).astype(jnp.bfloat16)
        head_part = inner_cols(query_hidden, fresh[2]).astype(jnp.bfloat16)
        heads[rows(target * step_rows, step_rows), :] = head_part
        for i in range(4):
            device = target * 4 + (inner + i) % 4
            source = heads.at[rows(device * block_rows, block_rows)]
            slot = len(copies)
            copy = remote(
                source,
                mixed.at[pair],
                head_send.at[slot],
                head_recv.at[pair],
                {"ctx": core, "hs": device},
            )
            condition = None
            if step == layers and i == 0:
                condition = helper

                @pl.when(owner)
                def _():
                    mixed[me] = source[...]

            guarded(condition, copy.start)
            copies.append((condition, copy))

    pl.when(owner)(cross)
    local[5].wait()
    for step in range(layers):
        for other_row in range(2):
            arrived(((depth + step) % layers) * 4 + ((row + other_row) % 2) * 2 + (1 - core))

    def head_arrived(index):
        remote(
            heads.at[pl.ds(0, block_rows)],
            mixed.at[index],
            head_send.at[0],
            head_recv.at[index],
            {"hs": core_peer},
        ).wait_recv()

    for step in range(1, count):
        head_arrived((me + step) % count)
    pl.when(helper)(functools.partial(head_arrived, me))

    for condition, copy in sends + copies:
        guarded(condition, copy.wait_send)
    for _, copy in crossed:
        copy.wait_send()

    @pl.when(helper)
    def _():
        for copy in outgoing + asked:
            copy.wait_send()

    @pl.when(owner)
    def _():
        for copy in handed:
            copy.wait_send()

    size = mixed.shape[2]
    head_count = side.shape[2] // size
    for seq in range(side.shape[1]):
        for head in range(head_count):
            columns = slice(head * size, (head + 1) * size)
            value = mixed[seq * head_count + head].astype(jnp.float32)
            square = jnp.mean(value * value, -1, keepdims=True)
            value = value * lax.rsqrt(square + epsilon) * gain_ref[:, columns]
            normed[seq * block_rows : (seq + 1) * block_rows, columns] = (
                value * opened[:, seq, columns]
            ).astype(jnp.bfloat16)
    result = jnp.dot(normed[...], full[...], preferred_element_type=jnp.float32)
    for seq in range(side.shape[1]):
        laid[:, seq, :] = result[seq * block_rows : (seq + 1) * block_rows]
    out_ref[...] = laid[...].astype(jnp.bfloat16)


def swapped_body(
    key_rows,
    value_rows,
    query_rows,
    step_rates,
    fast_gate,
    fast_up,
    fast_down,
    out_gain,
    gate_input,
    out_weight,
):
    layers = lax.axis_size("hs") // 4
    count = 4 * layers
    pieces = 2
    tokens, size = key_rows.shape[1:]
    hidden_size = 2 * fast_gate.shape[1]
    block_rows, seq_count, width = gate_input.shape
    columns = out_weight.shape[1]
    anywhere = pl.BlockSpec(memory_space=pl.ANY)
    inside = pl.BlockSpec(memory_space=pltpu.VMEM)
    half = jnp.bfloat16
    return pl.pallas_call(
        functools.partial(layer_kernel, layers, pieces),
        out_shape=jax.ShapeDtypeStruct((block_rows, seq_count, columns), half),
        in_specs=[anywhere] * 8 + [inside] * 2,
        out_specs=inside,
        scratch_shapes=[
            pltpu.VMEM((3, hidden_size, size), half),
            pltpu.VMEM((3, hidden_size, size), half),
            pltpu.VMEM((2 * tokens, size), half),
            pltpu.VMEM((2 * tokens, size), half),
            pltpu.VMEM((1, tokens), jnp.float32),
            pltpu.VMEM((tokens, size), half),
            pltpu.VMEM((block_rows, seq_count, width), half),
            pltpu.VMEM((block_rows, seq_count, width), jnp.float32),
            pltpu.VMEM((width, columns), half),
            pltpu.VMEM((3, hidden_size, size), jnp.float32),
            pltpu.VMEM((tokens, size), half),
            pltpu.VMEM((count, block_rows, size), half),
            pltpu.VMEM((seq_count * block_rows, width), half),
            pltpu.VMEM((block_rows, seq_count, columns), jnp.float32),
            pltpu.SemaphoreType.DMA((8,)),
            pltpu.SemaphoreType.DMA((4 + 2 * pieces + layers,)),
            pltpu.SemaphoreType.DMA((4 + 2 * pieces + layers,)),
            pltpu.SemaphoreType.DMA((4 + 6 * (layers - 1) + layers,)),
            pltpu.SemaphoreType.DMA((count,)),
            pltpu.SemaphoreType.DMA((count,)),
            pltpu.SemaphoreType.DMA((count,)),
            pltpu.SemaphoreType.DMA((3,)),
            pltpu.SemaphoreType.DMA((3,)),
        ],
        compiler_params=pltpu.CompilerParams(
            collective_id=0, has_side_effects=True, vmem_limit_bytes=60 * 1024 * 1024
        ),
    )(
        fast_gate,
        fast_up,
        fast_down,
        key_rows,
        value_rows,
        query_rows,
        gate_input,
        out_weight,
        step_rates,
        out_gain[None],
    )

def solution(mesh):
    def step(*arrays):
        paired = mesh.shape["ctx"] == 2 and mesh.shape["hs"] % 8 == 0
        paired = paired and arrays[0].shape[0] == 1
        return (swapped_body if paired else body)(*arrays)

    return jax.shard_map(
        step,
        mesh=mesh,
        in_specs=(
            P("hs", "ctx", None),
            P("hs", "ctx", None),
            P("hs", "ctx", None),
            P("hs", "ctx"),
            P("hs", "ctx", None),
            P("hs", "ctx", None),
            P("hs", "ctx", None),
            P(),
            P(("ctx", "hs"), None, None),
            P("hs", None),
        ),
        out_specs=P(("ctx", "hs"), None, None),
        check_vma=False,
    )
```

```python
import functools

import jax
import jax.numpy as jnp
from jax import lax
from jax.experimental import pallas as pl
from jax.experimental.pallas import tpu as pltpu
from jax.sharding import PartitionSpec as P

epsilon = 1e-06


def rescale_rows(weight, update):
    base = weight.astype(jnp.float32)
    moved = base + update
    factor = jnp.sqrt(jnp.mean(base * base, -1, keepdims=True) + epsilon) / jnp.sqrt(
        jnp.mean(moved * moved, -1, keepdims=True) + epsilon
    )
    return (moved * factor).astype(jnp.bfloat16)


def inner_rows(left, right):
    return lax.dot_general(
        left, right, (((0,), (0,)), ((), ())), preferred_element_type=jnp.float32
    )


def body(
    key_rows,
    value_rows,
    query_rows,
    step_rates,
    fast_gate,
    fast_up,
    fast_down,
    out_gain,
    gate_input,
    out_weight,
):
    key_row = key_rows[0]
    value_row = value_rows[0]
    query_row = query_rows[0]
    rate_row = step_rates[0]
    whole_gate, whole_up, whole_down = (
        lax.all_gather(fast_gate, "ctx", axis=1, tiled=True),
        lax.all_gather(fast_up, "ctx", axis=1, tiled=True),
        lax.all_gather(fast_down, "ctx", axis=1, tiled=True),
    )
    gate_fast = whole_gate[0]
    up_fast = whole_up[0]
    down_fast = whole_down[0]
    pre_gate = jnp.dot(key_row, gate_fast.T, preferred_element_type=jnp.float32)
    pre_up = jnp.dot(key_row, up_fast.T, preferred_element_type=jnp.float32)
    sig_gate = jax.nn.sigmoid(pre_gate)
    act_gate = pre_gate * sig_gate
    hidden = (act_gate * pre_up).astype(jnp.bfloat16)
    scaled = (rate_row[:, None] * value_row.astype(jnp.float32)).astype(jnp.bfloat16)
    grad_down = inner_rows(scaled, hidden)
    back_hidden = jnp.dot(scaled, down_fast, preferred_element_type=jnp.float32)
    back_gate = (back_hidden * pre_up * sig_gate * (1.0 + pre_gate * (1.0 - sig_gate))).astype(
        jnp.bfloat16
    )
    back_up = (back_hidden * act_gate).astype(jnp.bfloat16)
    grad_gate = inner_rows(back_gate, key_row)
    grad_up = inner_rows(back_up, key_row)
    grad_gate, grad_up, grad_down = (
        lax.psum_scatter(grad_gate, "ctx", scatter_dimension=0, tiled=True),
        lax.psum_scatter(grad_up, "ctx", scatter_dimension=0, tiled=True),
        lax.psum_scatter(grad_down, "ctx", scatter_dimension=0, tiled=True),
    )
    part_gate = rescale_rows(fast_gate[0], grad_gate)
    part_up = rescale_rows(fast_up[0], grad_up)
    part_down = rescale_rows(fast_down[0], grad_down)
    new_gate, new_up, new_down = (
        lax.all_gather(part_gate, "ctx", axis=0, tiled=True),
        lax.all_gather(part_up, "ctx", axis=0, tiled=True),
        lax.all_gather(part_down, "ctx", axis=0, tiled=True),
    )
    query_gate = jnp.dot(query_row, new_gate.T, preferred_element_type=jnp.float32)
    query_up = jnp.dot(query_row, new_up.T, preferred_element_type=jnp.float32)
    query_hidden = (jax.nn.silu(query_gate) * query_up).astype(jnp.bfloat16)
    head_out = jnp.dot(query_hidden, new_down.T, preferred_element_type=jnp.float32).astype(
        jnp.bfloat16
    )
    width_hs = lax.axis_size("hs")
    head_size = head_out.shape[1]
    token_count = head_out.shape[0] // width_hs
    blocks = head_out.reshape(width_hs, token_count, head_size)
    moved = lax.all_to_all(blocks, "hs", split_axis=0, concat_axis=2, tiled=True)
    seq_count = gate_input.shape[1]
    model_width = gate_input.shape[2]
    head_count = model_width // head_size
    mixed = moved.reshape(token_count, seq_count, head_count, head_size).astype(jnp.float32)
    square = jnp.mean(mixed * mixed, -1, keepdims=True)
    scaled_heads = mixed * lax.rsqrt(square + epsilon) * out_gain.reshape(head_count, head_size)
    normed = (
        scaled_heads.reshape(token_count, seq_count, model_width)
        * jax.nn.silu(gate_input.astype(jnp.float32))
    ).astype(jnp.bfloat16)
    flat_rows = normed.reshape(token_count * seq_count, model_width)
    out_cols = out_weight.shape[1]
    full_weight = lax.all_gather(out_weight, "hs", axis=0, tiled=True)
    result = jnp.dot(flat_rows, full_weight, preferred_element_type=jnp.float32)
    return result.astype(jnp.bfloat16).reshape(token_count, seq_count, out_cols)


MESH = pl.DeviceIdType.MESH


def inner_cols(left, right):
    return lax.dot_general(
        left, right, (((1,), (1,)), ((), ())), preferred_element_type=jnp.float32
    )


def layer_kernel(
    layers,
    pieces,
    gate_hbm,
    up_hbm,
    down_hbm,
    key_hbm,
    value_hbm,
    query_hbm,
    side_hbm,
    weight_hbm,
    rate_ref,
    gain_ref,
    out_ref,
    fast,
    fresh,
    keys,
    values,
    rates,
    queries,
    side,
    opened,
    full,
    grads,
    heads,
    mixed,
    normed,
    laid,
    local_sem,
    ctx_send,
    ctx_recv,
    full_send,
    full_recv,
    head_send,
    head_recv,
    fresh_send,
    fresh_recv,
):
    ctx = lax.axis_index("ctx")
    me = lax.axis_index("hs")
    other = 1 - ctx
    count = 4 * layers
    depth, inner = me // 4, me % 4
    row, core = inner // 2, inner % 2
    row_peer = depth * 4 + (1 - row) * 2 + core
    core_peer = depth * 4 + row * 2 + (1 - core)
    pair = depth * 4 + row * 2 + ctx
    owner = core == ctx
    helper = core != ctx

    def remote(source, target, send, recv, device):
        return pltpu.make_async_remote_copy(
            src_ref=source,
            dst_ref=target,
            send_sem=send,
            recv_sem=recv,
            device_id=device,
            device_id_type=MESH,
        )

    part = gate_hbm.shape[1]
    tokens = key_hbm.shape[1]
    piece = tokens // pieces
    shard = weight_hbm.shape[0]

    def rows(start, size):
        return pl.ds(pl.multiple_of(start, size), size)

    weights = (gate_hbm, up_hbm, down_hbm)
    local = []
    for i, source in enumerate(weights):
        local.append(
            pltpu.make_async_copy(source.at[0], fast.at[i, rows(ctx * part, part)], local_sem.at[i])
        )
    local.append(
        pltpu.make_async_copy(key_hbm.at[0], keys.at[rows(ctx * tokens, tokens)], local_sem.at[3])
    )
    local.append(
        pltpu.make_async_copy(value_hbm.at[0], values.at[rows(ctx * tokens, tokens)], local_sem.at[4])
    )
    local.append(pltpu.make_async_copy(weight_hbm, full.at[rows(me * shard, shard)], local_sem.at[5]))
    local.append(pltpu.make_async_copy(query_hbm.at[0], queries, local_sem.at[6]))
    local.append(pltpu.make_async_copy(side_hbm, side, local_sem.at[7]))
    owned = [0, 1, 2, 3, 4, 6]
    for i in (5, 7):
        local[i].start()

    @pl.when(owner)
    def _():
        for i in owned:
            local[i].start()

    barrier = pltpu.get_barrier_semaphore()
    pl.semaphore_signal(barrier, inc=1, device_id={"ctx": other}, device_id_type=MESH)
    for step in range(1, count):
        for side_ctx in (ctx, other):
            pl.semaphore_signal(
                barrier,
                inc=1,
                device_id={"ctx": side_ctx, "hs": (me + step) % count},
                device_id_type=MESH,
            )
    pl.semaphore_wait(barrier, 2 * count - 1)

    swaps = []
    for i, source in enumerate(weights):
        swaps.append((source.at[0], lambda who, i=i: fast.at[i, rows(who * part, part)]))
    for j in range(pieces):
        for source, target in ((key_hbm.at[0], keys), (value_hbm.at[0], values)):
            swaps.append(
                (
                    source.at[pl.ds(j * piece, piece)],
                    lambda who, target=target, j=j: target.at[
                        rows(who * tokens + j * piece, piece)
                    ],
                )
            )
    swaps.append((rate_ref, lambda who: rates))
    outgoing = [
        remote(source, target(ctx), ctx_send.at[i], ctx_recv.at[i], {"ctx": other})
        for i, (source, target) in enumerate(swaps)
    ]
    incoming = [
        remote(source, target(other), ctx_send.at[i], ctx_recv.at[i], {"ctx": other})
        for i, (source, target) in enumerate(swaps)
    ]
    block_rows = tokens // count
    step_rows = 4 * block_rows
    mid = layers // 2
    near = (depth // mid) * mid
    order = [mid - near + (depth + step) % mid for step in range(mid)]
    order += [near + (depth + step) % mid for step in range(1, mid)] + [depth]
    asked = []
    for step in range(layers):
        span = rows(order[step] * step_rows, step_rows)
        slot = len(swaps) + step
        asked.append(
            remote(
                query_hbm.at[0, span],
                queries.at[span],
                ctx_send.at[slot],
                ctx_recv.at[slot],
                {"ctx": other, "hs": core_peer},
            )
        )

    @pl.when(helper)
    def _():
        for copy in outgoing[-1:] + outgoing[:-1] + asked:
            copy.start()

    def full_copy(source, index, slot, device):
        return remote(
            source,
            full.at[rows(index * shard, shard)],
            full_send.at[slot],
            full_recv.at[index],
            {"hs": device},
        )

    def arrived(index):
        block = full.at[rows(index * shard, shard)]
        remote(block, block, full_send.at[0], full_recv.at[index], {"hs": core_peer}).wait_recv()

    def held(index):
        return full.at[rows(index * shard, shard)]

    sends = [
        (depth < layers - 1, full_copy(weight_hbm, me, 0, me + 4)),
        (depth > 0, full_copy(weight_hbm, me, 1, me - 4)),
        (None, full_copy(weight_hbm, me, 2, row_peer)),
        (None, full_copy(weight_hbm, me, 3, core_peer)),
    ]

    def guarded(condition, action):
        if condition is None:
            action()
        else:
            pl.when(condition)(action)

    for condition, copy in sends:
        guarded(condition, copy.start)

    def relay(hop):
        for turn, (exists, onward) in enumerate(
            (
                (depth >= hop, depth < layers - 1),
                (depth + hop <= layers - 1, depth > 0),
            )
        ):
            index = me - 4 * hop if turn == 0 else me + 4 * hop
            slot = 4 + ((hop - 1) * 2 + turn) * 3
            next_device = me + 4 if turn == 0 else me - 4
            made = [
                (exists & onward, full_copy(held(index), index, slot, next_device)),
                (exists, full_copy(held(index), index, slot + 1, row_peer)),
                (exists, full_copy(held(index), index, slot + 2, core_peer)),
            ]
            pl.when(exists)(functools.partial(arrived, index))
            for condition, copy in made:
                guarded(condition, copy.start)
            sends.extend(made)

    crossed = []
    for step in range(layers):
        index = ((depth + step) % layers) * 4 + (1 - row) * 2 + core
        slot = 4 + 6 * (layers - 1) + step
        crossed.append((index, full_copy(held(index), index, slot, core_peer)))

    def cross():
        for index, copy in crossed:
            arrived(index)
            copy.start()

    def learn(start, rate, first):
        key_part = keys[rows(start, piece), :]
        rate_column = jnp.broadcast_to(rate, (128, piece)).T[:, :1]
        scaled_part = (rate_column * values[rows(start, piece), :].astype(jnp.float32)).astype(
            jnp.bfloat16
        )
        pre_gate = inner_cols(key_part, fast[0])
        pre_up = inner_cols(key_part, fast[1])
        sig_gate = jax.nn.sigmoid(pre_gate)
        act_gate = pre_gate * sig_gate
        hidden = (act_gate * pre_up).astype(jnp.bfloat16)
        back_hidden = jnp.dot(scaled_part, fast[2], preferred_element_type=jnp.float32)
        back_gate = (
            back_hidden * pre_up * sig_gate * (1.0 + pre_gate * (1.0 - sig_gate))
        ).astype(jnp.bfloat16)
        back_up = (back_hidden * act_gate).astype(jnp.bfloat16)
        terms = (
            inner_rows(back_gate, key_part),
            inner_rows(back_up, key_part),
            inner_rows(scaled_part, hidden),
        )
        for i, term in enumerate(terms):
            grads[i] = term if first else grads[i] + term

    handed = [
        remote(fresh.at[i], fresh.at[i], fresh_send.at[i], fresh_recv.at[i], {"hs": core_peer})
        for i in range(3)
    ]
    local[7].wait()
    gate = side[...].astype(jnp.float32)
    opened[...] = gate * jax.nn.sigmoid(gate)
    hops = list(range(1, layers))
    if hops:
        relay(hops.pop(0))

    @pl.when(owner)
    def _():
        for i in owned[:5]:
            local[i].wait()
        for copy in incoming[:3]:
            copy.wait_recv()
        for j in range(pieces):
            learn(ctx * tokens + j * piece, rate_ref[:, j * piece : (j + 1) * piece], j == 0)

    for j in range(pieces):
        if hops:
            relay(hops.pop(0))

        @pl.when(owner)
        def _():
            if j == 0:
                incoming[-1].wait_recv()
            incoming[3 + 2 * j].wait_recv()
            incoming[4 + 2 * j].wait_recv()
            learn(other * tokens + j * piece, rates[:, j * piece : (j + 1) * piece], False)

    for hop in hops:
        relay(hop)

    @pl.when(owner)
    def _():
        for i in range(3):
            fresh[i] = rescale_rows(fast[i], grads[i])
            handed[i].start()
        local[6].wait()

    @pl.when(helper)
    def _():
        for copy in handed:
            copy.wait_recv()

    copies = []
    for step in range(1, layers + 1):
        target = order[step - 1]
        pl.when(helper)(asked[step - 1].wait_recv)
        query_part = queries[rows(target * step_rows, step_rows), :]
        query_gate = inner_cols(query_part, fresh[0])
        query_up = inner_cols(query_part, fresh[1])
        query_hidden = (query_gate * jax.nn.sigmoid(query_gate) * query_up).astype(jnp.bfloat16)
        head_part = inner_cols(query_hidden, fresh[2]).astype(jnp.bfloat16)
        heads[rows(target * step_rows, step_rows), :] = head_part
        for i in range(4):
            device = target * 4 + (inner + i) % 4
            source = heads.at[rows(device * block_rows, block_rows)]
            slot = len(copies)
            copy = remote(
                source,
                mixed.at[pair],
                head_send.at[slot],
                head_recv.at[pair],
                {"ctx": core, "hs": device},
            )
            condition = None
            if step == layers and i == 0:
                condition = helper

                @pl.when(owner)
                def _():
                    mixed[me] = source[...]

            guarded(condition, copy.start)
            copies.append((condition, copy))

    cross()
    local[5].wait()
    for step in range(layers):
        for other_row in range(2):
            arrived(((depth + step) % layers) * 4 + ((row + other_row) % 2) * 2 + (1 - core))

    def head_arrived(index):
        remote(
            heads.at[pl.ds(0, block_rows)],
            mixed.at[index],
            head_send.at[0],
            head_recv.at[index],
            {"hs": core_peer},
        ).wait_recv()

    for step in range(1, count):
        head_arrived((me + step) % count)
    pl.when(helper)(functools.partial(head_arrived, me))

    for condition, copy in sends + copies:
        guarded(condition, copy.wait_send)
    for _, copy in crossed:
        copy.wait_send()

    @pl.when(helper)
    def _():
        for copy in outgoing + asked:
            copy.wait_send()

    @pl.when(owner)
    def _():
        for copy in handed:
            copy.wait_send()

    size = mixed.shape[2]
    head_count = side.shape[2] // size
    for seq in range(side.shape[1]):
        for head in range(head_count):
            columns = slice(head * size, (head + 1) * size)
            value = mixed[seq * head_count + head].astype(jnp.float32)
            square = jnp.mean(value * value, -1, keepdims=True)
            value = value * lax.rsqrt(square + epsilon) * gain_ref[:, columns]
            normed[seq * block_rows : (seq + 1) * block_rows, columns] = (
                value * opened[:, seq, columns]
            ).astype(jnp.bfloat16)
    result = jnp.dot(normed[...], full[...], preferred_element_type=jnp.float32)
    for seq in range(side.shape[1]):
        laid[:, seq, :] = result[seq * block_rows : (seq + 1) * block_rows]
    out_ref[...] = laid[...].astype(jnp.bfloat16)


def swapped_body(
    key_rows,
    value_rows,
    query_rows,
    step_rates,
    fast_gate,
    fast_up,
    fast_down,
    out_gain,
    gate_input,
    out_weight,
):
    layers = lax.axis_size("hs") // 4
    count = 4 * layers
    pieces = 2
    tokens, size = key_rows.shape[1:]
    hidden_size = 2 * fast_gate.shape[1]
    block_rows, seq_count, width = gate_input.shape
    columns = out_weight.shape[1]
    anywhere = pl.BlockSpec(memory_space=pl.ANY)
    inside = pl.BlockSpec(memory_space=pltpu.VMEM)
    half = jnp.bfloat16
    return pl.pallas_call(
        functools.partial(layer_kernel, layers, pieces),
        out_shape=jax.ShapeDtypeStruct((block_rows, seq_count, columns), half),
        in_specs=[anywhere] * 8 + [inside] * 2,
        out_specs=inside,
        scratch_shapes=[
            pltpu.VMEM((3, hidden_size, size), half),
            pltpu.VMEM((3, hidden_size, size), half),
            pltpu.VMEM((2 * tokens, size), half),
            pltpu.VMEM((2 * tokens, size), half),
            pltpu.VMEM((1, tokens), jnp.float32),
            pltpu.VMEM((tokens, size), half),
            pltpu.VMEM((block_rows, seq_count, width), half),
            pltpu.VMEM((block_rows, seq_count, width), jnp.float32),
            pltpu.VMEM((width, columns), half),
            pltpu.VMEM((3, hidden_size, size), jnp.float32),
            pltpu.VMEM((tokens, size), half),
            pltpu.VMEM((count, block_rows, size), half),
            pltpu.VMEM((seq_count * block_rows, width), half),
            pltpu.VMEM((block_rows, seq_count, columns), jnp.float32),
            pltpu.SemaphoreType.DMA((8,)),
            pltpu.SemaphoreType.DMA((4 + 2 * pieces + layers,)),
            pltpu.SemaphoreType.DMA((4 + 2 * pieces + layers,)),
            pltpu.SemaphoreType.DMA((4 + 6 * (layers - 1) + layers,)),
            pltpu.SemaphoreType.DMA((count,)),
            pltpu.SemaphoreType.DMA((count,)),
            pltpu.SemaphoreType.DMA((count,)),
            pltpu.SemaphoreType.DMA((3,)),
            pltpu.SemaphoreType.DMA((3,)),
        ],
        compiler_params=pltpu.CompilerParams(
            collective_id=0, has_side_effects=True, vmem_limit_bytes=60 * 1024 * 1024
        ),
    )(
        fast_gate,
        fast_up,
        fast_down,
        key_rows,
        value_rows,
        query_rows,
        gate_input,
        out_weight,
        step_rates,
        out_gain[None],
    )

def solution(mesh):
    def step(*arrays):
        paired = mesh.shape["ctx"] == 2 and mesh.shape["hs"] % 8 == 0
        paired = paired and arrays[0].shape[0] == 1
        return (swapped_body if paired else body)(*arrays)

    return jax.shard_map(
        step,
        mesh=mesh,
        in_specs=(
            P("hs", "ctx", None),
            P("hs", "ctx", None),
            P("hs", "ctx", None),
            P("hs", "ctx"),
            P("hs", "ctx", None),
            P("hs", "ctx", None),
            P("hs", "ctx", None),
            P(),
            P(("ctx", "hs"), None, None),
            P("hs", None),
        ),
        out_specs=P(("ctx", "hs"), None, None),
        check_vma=False,
    )
```
